256 devices in a mesh: cross: 8 (over z_hi, core), strike: 32 (over z_lo, x, y).
Axes of the slice: x: 4, y: 4, z: 8 (z_hi: 4, z_lo: 2; z = z_hi * 2 + z_lo), core: 2. Of those that a mesh axis runs over, the one named last changes fastest.
Arguments:
- pressure: float32 [1024, 8, 4096], P('strike', 'cross'), may hold values from -6 to 6
- source: float32 [1024, 8, 4096], P('strike', 'cross'), may hold values from -6 to 6
- facies: int32 [1024, 8, 4096], P('strike', 'cross'), may hold values from 0 to 7
- mobility_table: float32 [8], replicated, may hold values from 0.3 to 3
Outputs:
- pressure_out: float32 [1024, 8, 4096], P('strike', 'cross')
- defect: float32 [1024, 8, 4096], P('strike', 'cross')
The draws below stay inside these ranges and needn't reach their ends.
All inputs are finite; a program needn't handle non-finite values.
Results may differ from the reference program's by a relative error of at most 0.0003.
Values sent between devices are 32-bit elements; how exact they have to be, the bound alone decides.
No kernel may reach another device: no remote copies, remote signals or barrier semaphores. Data moves between devices by JAX's collectives and lax.ppermute only.
A program may use at most 64 MiB of HBM per device.

```python
import math
import jax
import jax.numpy as jnp
from jax import lax

ND = 1024
CLASSES = 8
DEFECT = 2
SWEEPS = 3
NC = 8
NS = 4096


def place_ends(array, own_key, least, high):
    extent = array.shape
    place = [jax.random.randint(jax.random.fold_in(own_key, axis), (), 0, extent[axis]) for axis in range(len(extent))]
    array = array.at[tuple(place)].set(least)
    longest = extent.index(max(extent))
    place[longest] = (place[longest] + 1) % extent[longest]
    return array.at[tuple(place)].set(high)


def block_levels(rng, extent, split, smallest, largest):
    gain = 1.0
    for dim, blocks in split:
        heights = jax.random.uniform(jax.random.fold_in(jax.random.fold_in(rng, 6), dim), (blocks,), jnp.float32, smallest / len(split), largest / len(split))
        gain = gain * jnp.repeat(jnp.exp(heights), extent[dim] // blocks).reshape((-1,) + (1,) * (len(extent) - 1 - dim))
    return gain


def centred(rng, extent, scale, bound, shards=(), kind=jnp.bfloat16):
    entries = scale * jax.random.normal(rng, extent, jnp.float32)
    if shards:
        entries = entries * block_levels(rng, extent, shards, -0.22, 0.18)
    return jnp.clip(entries, -bound, bound).astype(kind)


def setup_inputs(seed: int = 0) -> dict:
    key_of = jax.random.split(jax.random.key(seed), 5)
    pressure = centred(key_of[0], (ND, NC, NS), 1.0, 6.0, ((0, 32), (1, 8)), jnp.float32)
    source = centred(key_of[1], (ND, NC, NS), 1.0, 6.0, ((0, 32), (1, 8)), jnp.float32)
    facies = place_ends(jax.random.randint(key_of[2], (ND, NC, NS), 0, CLASSES), jax.random.fold_in(key_of[2], 1), 0, CLASSES - 1).astype(jnp.int32)
    mobility_table = jnp.clip(jnp.exp(jax.random.uniform(key_of[3], (CLASSES,), jnp.float32, math.log(0.3), math.log(3.0))), 0.3, 3.0)
    return dict(pressure=pressure, source=source, facies=facies, mobility_table=mobility_table)


STORE = 0.5
LOW = 0.05
HIGH = 1.95

def chebyshev_weights(count):
    middle = 0.5 * (LOW + HIGH)
    half = 0.5 * (HIGH - LOW)
    return [1.0 / (middle + half * math.cos(math.pi * (2 * j + 1) / (2 * count))) for j in range(count)]

def neighbour(padded, axis, offset, shape):
    starts = [1, 1, 1]
    starts[axis] = offset
    limits = [s + n for s, n in zip(starts, shape)]
    return lax.slice(padded, starts, limits)

def operate_padded(field, mobile, padded_f, padded_m):
    total = STORE * field
    for axis in range(3):
        for offset in (0, 2):
            near_f = neighbour(padded_f, axis, offset, field.shape)
            near_m = neighbour(padded_m, axis, offset, field.shape)
            total = total + 0.5 * (mobile + near_m) * (field - near_f)
    return total

def lookup(classes, table):
    base = jnp.zeros(classes.shape, table.dtype)
    for code in range(CLASSES):
        base = jnp.where(classes == code, table[code], base)
    return base

def forward_plane(plane):
    count = plane.shape[0]
    whole = jnp.concatenate([plane, plane[::-1]], axis=0)
    spectrum = jnp.fft.fft(whole, axis=0)[:count]
    wave = jnp.arange(count).astype(plane.dtype)
    twist = jnp.exp(-1j * jnp.pi * wave / (2 * count))
    scale = jnp.where(wave == 0, jnp.sqrt(1.0 / count), jnp.sqrt(2.0 / count)).astype(plane.dtype)
    return (scale[:, None] * 0.5 * jnp.real(twist[:, None] * spectrum)).astype(plane.dtype)

def inverse_plane(coeffs):
    count = coeffs.shape[0]
    wave = jnp.arange(count).astype(coeffs.dtype)
    twist = jnp.exp(1j * jnp.pi * wave / (2 * count))
    scale = jnp.where(wave == 0, jnp.sqrt(1.0 / count), jnp.sqrt(2.0 / count)).astype(coeffs.dtype)
    spread = scale[:, None] * coeffs * twist[:, None]
    padded = jnp.concatenate([spread, jnp.zeros_like(spread)], axis=0)
    values = jnp.fft.ifft(padded, axis=0) * (2 * count)
    return jnp.real(values[:count]).astype(coeffs.dtype)

def along_dip(function, field):
    planes = jnp.moveaxis(field, 1, 0)
    return jnp.moveaxis(lax.map(function, planes), 0, 1)

def plane_sweeps(rhat, mref):
    count = rhat.shape[0]
    omega = chebyshev_weights(SWEEPS)
    lam = (2.0 - 2.0 * jnp.cos(jnp.pi * jnp.arange(count).astype(rhat.dtype) / count))[:, None, None]
    diag = STORE + mref * (lam + 4.0)
    answer = omega[0] * rhat / diag
    for step in range(1, SWEEPS):
        padded = jnp.pad(answer, ((0, 0), (1, 1), (1, 1)))
        near = padded[:, :-2, 1:-1] + padded[:, 2:, 1:-1] + padded[:, 1:-1, :-2] + padded[:, 1:-1, 2:]
        answer = answer + omega[step] * (rhat - (diag * answer - mref * near)) / diag
    return answer

def reference(pressure, source, facies, mobility_table):
    base = lookup(facies, mobility_table)
    field = pressure
    defect = jnp.zeros_like(pressure)
    for step in range(DEFECT):
        mobile = base * (1.0 + 0.5 * jnp.tanh(field))
        residual = source - operate_padded(field, mobile, jnp.pad(field, 1), jnp.pad(mobile, 1))
        defect = residual
        rhat = along_dip(forward_plane, residual)
        mref = lax.optimization_barrier(jnp.mean(mobile, axis=0, keepdims=True))
        answer = plane_sweeps(rhat, mref)
        field = field + along_dip(inverse_plane, answer)
    return (field, defect)
```

```python
import math

import jax
import jax.numpy as jnp
from jax import lax
from jax.experimental import pallas as pl
from jax.experimental.pallas import tpu as pltpu
from jax.sharding import PartitionSpec as P

ND = 1024
CLASSES = 8
DEFECT = 2
SWEEPS = 3

STORE = 0.5
LOW = 0.05
HIGH = 1.95

LANES = 128
BLOCKS = 32
ROWS = ND // BLOCKS
GROUP = 16
AXES = ("cross", "strike")
FIELDS = 3
HALF = 2 * FIELDS


def chebyshev_weights(count):
    middle = 0.5 * (LOW + HIGH)
    half = 0.5 * (HIGH - LOW)
    return [
        1.0 / (middle + half * math.cos(math.pi * (2 * j + 1) / (2 * count))) for j in range(count)
    ]


def device_of(chunk):
    row, q = divmod(chunk, 8)
    return 64 * (row // 8) + 4 * (row % 8) + 32 * (q % 2) + q // 2


def exchange(vectors, keep=None):
    block = lax.broadcasted_iota(jnp.int32, vectors[0].shape, 1) // 8
    for step in (1, 8, 4, 2):
        high = (block & step) != 0
        done = []
        for b in range(GROUP):
            if step == 2 and keep is not None and b not in keep:
                done.append(None)
            elif b & step:
                other = pltpu.roll(vectors[b ^ step], LANES - 8 * step, 1)
                done.append(jnp.where(high, vectors[b], other))
            else:
                other = pltpu.roll(vectors[b ^ step], 8 * step, 1)
                done.append(jnp.where(high, other, vectors[b]))
        vectors = done
    return vectors


def pack_kernel(table, pressure, source, facies, out):
    def body(g, carry):
        tile, upper = g // 2, g % 2

        def read(ref):
            return [ref[pl.ds((upper * GROUP + b) * 32 + tile * 8, 8), :] for b in range(GROUP)]

        def lookup(codes):
            base = jnp.zeros(codes.shape, jnp.float32)
            for code in range(CLASSES):
                base = jnp.where(codes == code, table[code], base)
            return base

        fields = (read(pressure), [lookup(c) for c in read(facies)], read(source))
        for k, vectors in enumerate(fields):
            moved = exchange(vectors)
            for b in range(GROUP):
                first = 64 * tile + 32 * ((b >> 1) & 1) + (b >> 2)
                row = first * 2 * HALF + (b & 1) * HALF + k * 2 + upper
                out[pl.ds(row, 8, stride=8 * HALF), :] = moved[b]
        return carry

    lax.fori_loop(0, 8, body, 0)


def halves_kernel(recv, lower, upper):
    def body(g, carry):
        for w in range(HALF):
            rows = pl.ds(w * 256 + g * 8, 8)
            lower[rows, :] = recv[pl.ds(g * 8 * 2 * HALF + w, 8, stride=2 * HALF), :]
            upper[rows, :] = recv[pl.ds(g * 8 * 2 * HALF + HALF + w, 8, stride=2 * HALF), :]
        return carry

    lax.fori_loop(0, 32, body, 0)


def roll_lanes(x, shift):
    return pltpu.roll(x.reshape(64, LANES), shift % LANES, 1).reshape(x.shape)


def shift_blocks(x, shift):
    row = lax.broadcasted_iota(jnp.int32, (BLOCKS, LANES), 0)
    keep = (row >= shift) if shift > 0 else (row < BLOCKS + shift)
    parts = [
        jnp.where(keep, pltpu.roll(x[h].reshape(BLOCKS, LANES), shift % BLOCKS, 0), 0.0) for h in range(2)
    ]
    return jnp.stack(parts).reshape(x.shape)


def sides(x):
    lane = lax.broadcasted_iota(jnp.int32, (4, 8, LANES), 2)
    low, high = lane < 32, lane >= 96
    zero = jnp.zeros((4, 8, LANES), jnp.float32)
    r, l = roll_lanes(x, 32), roll_lanes(x, -32)
    left = jnp.stack([jnp.where(low, zero, r[0]), jnp.where(low, r[0], r[1])])
    right = jnp.stack([jnp.where(high, l[1], l[0]), jnp.where(high, zero, l[1])])
    return left, right, roll_lanes(x, 1), roll_lanes(x, -1)


def column_sum(x):
    total = jnp.sum(x, axis=(1, 2), keepdims=True)
    return jnp.broadcast_to(total, (2, 1, 8, LANES))


def work_kernel(own, left_halo, right_halo, out, p, m, base, source, resid, rho, part, power):
    omega = chebyshev_weights(SWEEPS)
    fields = (p, base, source)

    def unpack(g, carry):
        upper, h, tile = g // 8, (g // 4) % 2, g % 4
        for k in range(FIELDS):
            vectors = []
            w = k * 2 + upper
            for c in range(4):
                block = (4 * h + c) * 32 + tile * 8
                vectors.append(left_halo[pl.ds(w * 256 + block, 8), :])
                vectors.append(own[pl.ds(block * 2 * HALF + w, 8, stride=2 * HALF), :])
                vectors.append(own[pl.ds(block * 2 * HALF + HALF + w, 8, stride=2 * HALF), :])
                vectors.append(right_halo[pl.ds(w * 256 + block, 8), :])
            moved = exchange(vectors)
            for b in range(GROUP):
                fields[k][upper * GROUP + b + 1, h, tile] = moved[b]
        return carry

    lax.fori_loop(0, 16, unpack, 0)

    slab = (2, 4, 8, LANES)
    zero = jnp.zeros(slab, jnp.float32)

    def mobility(i, field):
        value = base[i + 1] * (1.0 + 0.5 * jnp.tanh(field))
        m[i + 1] = value
        return value

    total = lax.fori_loop(0, ROWS, lambda i, acc: acc + mobility(i, p[i + 1]), zero)

    for step in range(DEFECT):
        for ref in (p, m):
            ref[0] = shift_blocks(ref[ROWS], 1)
            ref[ROWS + 1] = shift_blocks(ref[1], -1)

        mref = column_sum(total) * (1.0 / ND)
        inside = mref > 0.0
        safe = jnp.where(inside, mref, 1.0)
        half = 0.5 * (4.0 + STORE / safe)
        ratio = 1.0 / (1.0 + half + jnp.sqrt(half * (half + 2.0)))
        gain = ratio / ((1.0 - ratio * ratio) * safe)

        def powers(i, value):
            value = value * ratio
            power[i] = value
            return value

        block_ratio = lax.fori_loop(0, ROWS, powers, jnp.ones((2, 1, 8, LANES), jnp.float32))
        squares = [block_ratio]
        for _ in range(5):
            squares.append(squares[-1] * squares[-1])
        whole = squares[5]
        reflect = 1.0 / (1.0 - whole * whole)
        index = lax.broadcasted_iota(jnp.int32, slab, 1) * 8 + lax.broadcasted_iota(jnp.int32, slab, 2)
        from_left = jnp.ones(slab, jnp.float32)
        from_right = jnp.ones(slab, jnp.float32)
        for bit in range(5):
            on = ((index >> bit) & 1) != 0
            from_left = jnp.where(on, from_left * squares[bit], from_left)
            from_right = jnp.where(on, from_right, from_right * squares[bit])

        def last(x, d):
            picked = jnp.where(index == d, x, 0.0)
            return column_sum(picked)

        def carries(ends, heads):
            for bit in range(5):
                ends = ends + squares[bit] * shift_blocks(ends, 1 << bit)
                heads = heads + squares[bit] * shift_blocks(heads, -(1 << bit))
            a, b = last(heads, 0), last(ends, BLOCKS - 1)
            before = shift_blocks(ends, 1) + from_left * ((a + whole * b) * reflect)
            after = shift_blocks(heads, -1) + from_right * ((b + whole * a) * reflect)
            return before, after

        def backward(values):
            def body(n, z):
                i = ROWS - 1 - n
                part[i] = part[i] + z
                return ratio * (values[i] + z)

            z = lax.fori_loop(0, ROWS - 1, body, zero, unroll=2)
            part[0] = part[0] + z
            return values[0] + z

        def form(i, y):
            here, mob = p[i + 1], m[i + 1]
            result = source[i + 1] - STORE * here
            near = [(p[i], m[i]), (p[i + 2], m[i + 2])] + list(zip(sides(here), sides(mob)))
            for other, other_m in near:
                result = result - 0.5 * (mob + other_m) * (here - other)
            result = jnp.where(inside, result, 0.0)
            resid[i] = result
            y = result + ratio * y
            part[i] = y
            return y

        ends = lax.fori_loop(0, ROWS, form, zero)
        values = resid
        for sweep in range(SWEEPS):
            before, after = carries(ends, backward(values))
            weight = omega[sweep]

            def solved(i):
                v = gain * (part[i] + power[i] * before + power[ROWS - 1 - i] * after)
                field = p[i + 1] + weight * v
                p[i + 1] = field
                return v, field

            if sweep + 1 < SWEEPS:
                previous, scaled = values, weight * mref

                def advance(i, y):
                    v, _ = solved(i)
                    a, b, c, d = sides(v)
                    value = (1.0 - weight) * previous[i] + scaled * (a + b + c + d)
                    rho[i] = value
                    y = value + ratio * y
                    part[i] = y
                    return y

                ends = lax.fori_loop(0, ROWS, advance, zero)
                values = rho
            elif step + 1 < DEFECT:
                total = lax.fori_loop(0, ROWS, lambda i, acc: acc + mobility(i, solved(i)[1]), zero)
            else:

                def finish(i, carry):
                    solved(i)
                    return carry

                lax.fori_loop(0, ROWS, finish, 0)

    kept = tuple(4 * c + s for c in range(4) for s in (1, 2))

    def pack(g, carry):
        upper, h, tile = g // 8, (g // 4) % 2, g % 4
        for k, (ref, offset) in enumerate(((p, 1), (resid, 0))):
            moved = exchange([ref[upper * GROUP + b + offset, h, tile] for b in range(GROUP)], kept)
            for c in range(4):
                block = (4 * h + c) * 32 + tile * 8
                for s in range(2):
                    row = block * 8 + s * 4 + k * 2 + upper
                    out[pl.ds(row, 8, stride=8), :] = moved[4 * c + 1 + s]
        return carry

    lax.fori_loop(0, 16, pack, 0)


def unpack_kernel(recv, pressure, defect):
    def body(g, carry):
        tile, upper = g // 2, g % 2
        for k, ref in enumerate((pressure, defect)):
            vectors = []
            for b in range(GROUP):
                first = 64 * tile + 32 * ((b >> 1) & 1) + (b >> 2)
                row = first * 8 + (b & 1) * 4 + k * 2 + upper
                vectors.append(recv[pl.ds(row, 8, stride=32), :])
            moved = exchange(vectors)
            for b in range(GROUP):
                ref[pl.ds((upper * GROUP + b) * 32 + tile * 8, 8), :] = moved[b]
        return carry

    lax.fori_loop(0, 8, body, 0)


def shape(rows):
    return jax.ShapeDtypeStruct((rows, LANES), jnp.float32)


VMEM = pl.BlockSpec(memory_space=pltpu.VMEM)
SMEM = pl.BlockSpec(memory_space=pltpu.SMEM)


def per_device(pressure, source, facies, mobility_table):
    flat = [x.reshape(ND, LANES) for x in (pressure, source, facies)]
    sent = pl.pallas_call(
        pack_kernel,
        out_shape=shape(3072),
        in_specs=[SMEM, VMEM, VMEM, VMEM],
        out_specs=VMEM,
        name="pack",
    )(mobility_table, *flat)
    recv = lax.all_to_all(sent.reshape(256, FIELDS, 4, LANES), AXES, 0, 0, tiled=True).reshape(3072, LANES)
    lower, upper = pl.pallas_call(
        halves_kernel,
        out_shape=(shape(1536), shape(1536)),
        in_specs=[VMEM],
        out_specs=(VMEM, VMEM),
        name="halves",
    )(recv)
    chain = [device_of(t) for t in range(256)]
    right_halo = lax.ppermute(lower, AXES, list(zip(chain[1:], chain[:-1])))
    left_halo = lax.ppermute(upper, AXES, list(zip(chain[:-1], chain[1:])))

    def cells(count):
        return pltpu.VMEM((count, 2, 4, 8, LANES), jnp.float32)

    result = pl.pallas_call(
        work_kernel,
        out_shape=shape(2048),
        in_specs=[VMEM, VMEM, VMEM],
        out_specs=VMEM,
        scratch_shapes=[
            cells(ROWS + 2),
            cells(ROWS + 2),
            cells(ROWS + 2),
            cells(ROWS + 2),
            cells(ROWS),
            cells(ROWS),
            cells(ROWS),
            pltpu.VMEM((ROWS, 2, 1, 8, LANES), jnp.float32),
        ],
        name="work",
    )(recv, left_halo, right_halo)
    back = lax.all_to_all(result.reshape(256, 8, LANES), AXES, 0, 0, tiled=True).reshape(2048, LANES)
    outs = pl.pallas_call(
        unpack_kernel,
        out_shape=(shape(ND), shape(ND)),
        in_specs=[VMEM],
        out_specs=(VMEM, VMEM),
        name="unpack",
    )(back)
    return tuple(x.reshape(pressure.shape) for x in outs)


def solution(mesh):
    spec = P("strike", "cross", None)
    return jax.shard_map(
        per_device,
        mesh=mesh,
        in_specs=(spec, spec, spec, P()),
        out_specs=(spec, spec),
        check_vma=False,
    )
```

```python
import math

import jax
import jax.numpy as jnp
from jax import lax
from jax.experimental import pallas as pl
from jax.experimental.pallas import tpu as pltpu
from jax.sharding import PartitionSpec as P

ND = 1024
CLASSES = 8
DEFECT = 2
SWEEPS = 3

STORE = 0.5
LOW = 0.05
HIGH = 1.95

LANES = 128
BLOCKS = 32
ROWS = ND // BLOCKS
GROUP = 16
AXES = ("cross", "strike")
FIELDS = 3
HALF = 2 * FIELDS


def chebyshev_weights(count):
    middle = 0.5 * (LOW + HIGH)
    half = 0.5 * (HIGH - LOW)
    return [
        1.0 / (middle + half * math.cos(math.pi * (2 * j + 1) / (2 * count))) for j in range(count)
    ]


def device_of(chunk):
    row, q = divmod(chunk, 8)
    z, s = divmod(row, 8)
    if s % 2:
        q = 7 - q
    place = s if s < 4 else 11 - s
    return 64 * z + 4 * place + 32 * (q % 2) + q // 2


def exchange(vectors, keep=range(GROUP)):
    block = lax.broadcasted_iota(jnp.int32, vectors[0].shape, 1) // 8
    vectors = [pltpu.roll(vectors[k], 8 * k, 1) if k else vectors[k] for k in range(GROUP)]
    vectors = [vectors[-k % GROUP] for k in range(GROUP)]
    for step in (1, 2, 4):
        here = (block & step) != 0
        vectors = [jnp.where(here, vectors[(k - step) % GROUP], vectors[k]) for k in range(GROUP)]
    here = block >= 8
    done = {}
    for b in keep:
        moved = jnp.where(here, vectors[(b - 8) % GROUP], vectors[b])
        done[b] = pltpu.roll(moved, LANES - 8 * b, 1) if b else moved
    return done


def snake_sublanes(vectors):
    row = lax.broadcasted_iota(jnp.int32, (8, LANES), 0)
    order = jnp.where(row < 4, row, 11 - row)
    return [jnp.take_along_axis(v, order, axis=0) for v in vectors]


def snake_chunks(vectors):
    row = lax.broadcasted_iota(jnp.int32, (8, LANES), 0)
    odd = ((row & 1) ^ (row >> 2)) != 0
    return [
        jnp.where(odd, vectors[GROUP - 2 - (k & -2) + (k & 1)], vectors[k]) for k in range(GROUP)
    ]


def pack_kernel(table, pressure, source, facies, out):
    def lookup(codes):
        base = jnp.zeros(codes.shape, jnp.float32)
        for code in range(CLASSES):
            base = jnp.where(codes == code, table[code], base)
        return base

    def body(upper, carry):
        def read(ref):
            return [ref[upper * GROUP + b] for b in range(GROUP)]

        fields = (read(pressure), [lookup(c) for c in read(facies)], read(source))
        for k, vectors in enumerate(fields):
            moved = snake_chunks(exchange(snake_sublanes(vectors)))
            for b in range(GROUP):
                row = (32 * ((b >> 1) & 1) + (b >> 2)) * 2 * HALF + (b & 1) * HALF + k * 2 + upper
                out[pl.ds(row, 8, stride=8 * HALF), :] = moved[b]
        return carry

    lax.fori_loop(0, 2, body, 0)


def halves_kernel(recv, lower, upper):
    def body(g, carry):
        for w in range(HALF):
            rows = pl.ds(w * 256 + g * 8, 8)
            lower[rows, :] = recv[pl.ds(g * 8 * 2 * HALF + w, 8, stride=2 * HALF), :]
            upper[rows, :] = recv[pl.ds(g * 8 * 2 * HALF + HALF + w, 8, stride=2 * HALF), :]
        return carry

    lax.fori_loop(0, 32, body, 0)


SLAB = (8, 8, LANES)


def roll_lanes(x, shift):
    return pltpu.roll(x.reshape(64, LANES), shift % LANES, 1).reshape(x.shape)


def shift_blocks(x, shift):
    lane = lax.broadcasted_iota(jnp.int32, SLAB, 2)
    if abs(shift) >= 8:
        lanes = shift * 4
        keep = (lane >= lanes) if shift > 0 else (lane < LANES + lanes)
        return jnp.where(keep, roll_lanes(x, lanes), 0.0)
    sub = lax.broadcasted_iota(jnp.int32, SLAB, 1)
    near = jnp.stack([pltpu.roll(x[c], shift % 8, 0) for c in range(8)])
    if shift > 0:
        far = jnp.where(lane >= 32, roll_lanes(near, 32), 0.0)
        return jnp.where(sub >= shift, near, far)
    far = jnp.where(lane < 96, roll_lanes(near, -32), 0.0)
    return jnp.where(sub < 8 + shift, near, far)


def column_sum(x):
    total = jnp.broadcast_to(jnp.sum(x, axis=1, keepdims=True), SLAB)
    total = total + roll_lanes(total, 32)
    return total + roll_lanes(total, 64)


def roll_sublanes(x, shift):
    return jnp.stack([pltpu.roll(x[c], shift % 8, 0) for c in range(8)])


def work_kernel(own, left_halo, right_halo, out, p, m, base, source, resid, rho, part, power):
    omega = chebyshev_weights(SWEEPS)
    fields = (p, base, source)

    def unpack(g, carry):
        upper, c = g // 8, g % 8
        for k in range(FIELDS):
            vectors = []
            w = k * 2 + upper
            for tile in range(4):
                block = c * 32 + tile * 8
                vectors.append(left_halo[pl.ds(w * 256 + block, 8), :])
                vectors.append(own[pl.ds(block * 2 * HALF + w, 8, stride=2 * HALF), :])
                vectors.append(own[pl.ds(block * 2 * HALF + HALF + w, 8, stride=2 * HALF), :])
                vectors.append(right_halo[pl.ds(w * 256 + block, 8), :])
            moved = exchange(vectors)
            for b in range(GROUP):
                fields[k][upper * GROUP + b + 1, c] = moved[b]
        return carry

    lax.fori_loop(0, 16, unpack, 0)

    zero = jnp.zeros(SLAB, jnp.float32)
    edge = jnp.zeros((1, 8, LANES), jnp.float32)
    lane = lax.broadcasted_iota(jnp.int32, SLAB, 2)
    sub = lax.broadcasted_iota(jnp.int32, SLAB, 1)

    def mobility(i, field):
        value = base[i + 1] * (1.0 + 0.5 * jnp.tanh(field))
        m[i + 1] = value
        return value

    total = lax.fori_loop(0, ROWS, lambda i, acc: acc + mobility(i, p[i + 1]), zero, unroll=2)

    for step in range(DEFECT):
        for ref in (p, m):
            ref[0] = shift_blocks(ref[ROWS], 1)
            ref[ROWS + 1] = shift_blocks(ref[1], -1)

        mref = column_sum(total) * (1.0 / ND)
        inside = mref > 0.0
        safe = jnp.where(inside, mref, 1.0)
        half = 0.5 * (4.0 + STORE / safe)
        ratio = 1.0 / (1.0 + half + jnp.sqrt(half * (half + 2.0)))
        gain = ratio / ((1.0 - ratio * ratio) * safe)
        inner = gain * mref
        gain = jnp.where(inside, gain, 0.0)

        def powers(i, value):
            power[i] = value
            return value * ratio

        block_ratio = lax.fori_loop(0, ROWS, powers, jnp.ones(SLAB, jnp.float32), unroll=2)
        power[ROWS] = block_ratio
        squares = [block_ratio]
        for _ in range(5):
            squares.append(squares[-1] * squares[-1])
        whole = squares[5]
        reflect = 1.0 / (1.0 - whole * whole)
        below_sub = jnp.ones(SLAB, jnp.float32)
        above_sub = jnp.ones(SLAB, jnp.float32)
        for bit in range(3):
            on = ((sub >> bit) & 1) != 0
            below_sub = jnp.where(on, below_sub * squares[bit], below_sub)
            above_sub = jnp.where(on, above_sub, above_sub * squares[bit])
        from_left, from_right = below_sub, above_sub
        for bit in range(2):
            on = ((lane >> (5 + bit)) & 1) != 0
            from_left = jnp.where(on, from_left * squares[3 + bit], from_left)
            from_right = jnp.where(on, from_right, from_right * squares[3 + bit])

        def spread(x, kept):
            x = jnp.where(kept, x, 0.0)
            x = x + roll_lanes(x, 32)
            return x + roll_lanes(x, 64)

        def carries(ends, heads):
            for bit in range(3):
                s = 1 << bit
                ends = ends + squares[bit] * jnp.where(sub >= s, roll_sublanes(ends, s), 0.0)
                heads = heads + squares[bit] * jnp.where(sub < 8 - s, roll_sublanes(heads, -s), 0.0)
            end = jnp.broadcast_to(ends[:, 7:8], SLAB)
            head = jnp.broadcast_to(heads[:, 0:1], SLAB)
            before, after = shift_blocks(end, 8), shift_blocks(head, -8)
            before = before + squares[3] * shift_blocks(before, 8)
            after = after + squares[3] * shift_blocks(after, -8)
            before = before + squares[4] * shift_blocks(before, 16)
            after = after + squares[4] * shift_blocks(after, -16)
            a = spread(head + squares[3] * after, lane < 32)
            b = spread(end + squares[3] * before, lane >= 96)
            before = jnp.where(sub > 0, roll_sublanes(ends, 1), 0.0) + below_sub * before
            after = jnp.where(sub < 7, roll_sublanes(heads, -1), 0.0) + above_sub * after
            before = before + from_left * ((a + whole * b) * reflect)
            after = after + from_right * ((b + whole * a) * reflect)
            return before, after

        def form(i, carry):
            y, other, above = carry
            here, mob = p[i + 1], m[i + 1]
            below = (mob + m[i + 2]) * (here - p[i + 2])
            flow = below - above
            wide, wide_m = jnp.concatenate([edge, here, edge]), jnp.concatenate([edge, mob, edge])
            across = (wide_m[:-1] + wide_m[1:]) * (wide[:-1] - wide[1:])
            flow = flow + (across[1:] - across[:-1])
            along = (mob + roll_lanes(mob, -1)) * (here - roll_lanes(here, -1))
            flow = flow + (along - roll_lanes(along, 1))
            result = source[i + 1] - STORE * here - 0.5 * flow
            if step + 1 == DEFECT:
                resid[i] = result
            value = gain * result
            rho[i] = value
            y = value + ratio * y
            part[i] = y
            return y, other + power[i] * value, below

        first = (m[0] + m[1]) * (p[0] - p[1])
        ends, heads, _ = lax.fori_loop(0, ROWS, form, (zero, zero, first), unroll=2)
        for sweep in range(SWEEPS):
            before, after = carries(ends, heads)
            down = sweep % 2 == 0
            entering, stored = (after, before) if down else (before, after)
            weight = omega[sweep]

            def solved(n, running):
                i = ROWS - 1 - n if down else n
                value = rho[i]
                opposite = ratio * running
                v = part[i] + power[ROWS - n] * stored + opposite
                field = p[i + 1] + weight * v
                p[i + 1] = field
                return i, value, value + opposite, v, field

            if sweep + 1 < SWEEPS:
                scaled = weight * inner

                def advance(n, carry):
                    running, x, other = carry
                    i, value, running, v, _ = solved(n, running)
                    near = roll_lanes(v, 1) + roll_lanes(v, -1)
                    near = near + (jnp.concatenate([edge, v[:-1]]) + jnp.concatenate([v[1:], edge]))
                    value = scaled * near if weight == 1.0 else (1.0 - weight) * value + scaled * near
                    rho[i] = value
                    x = value + ratio * x
                    part[i] = x
                    return running, x, other + power[n] * value

                _, x, other = lax.fori_loop(0, ROWS, advance, (entering, zero, zero), unroll=2)
                ends, heads = (other, x) if down else (x, other)
            elif step + 1 < DEFECT:

                def renew(n, carry):
                    running, acc = carry
                    i, _, running, _, field = solved(n, running)
                    return running, acc + mobility(i, field)

                total = lax.fori_loop(0, ROWS, renew, (entering, zero), unroll=2)[1]
            else:
                lax.fori_loop(0, ROWS, lambda n, running: solved(n, running)[2], entering, unroll=2)

    kept = tuple(4 * tile + s for tile in range(4) for s in (1, 2))

    def pack(g, carry):
        upper, c = g // 8, g % 8
        for k, (ref, offset) in enumerate(((p, 1), (resid, 0))):
            moved = exchange([ref[upper * GROUP + b + offset, c] for b in range(GROUP)], kept)
            for tile in range(4):
                for s in range(2):
                    row = (c * 32 + tile * 8) * 8 + s * 4 + k * 2 + upper
                    out[pl.ds(row, 8, stride=8), :] = moved[4 * tile + 1 + s]
        return carry

    lax.fori_loop(0, 16, pack, 0)


def unpack_kernel(recv, pressure, defect):
    def body(upper, carry):
        for k, ref in enumerate((pressure, defect)):
            vectors = []
            for b in range(GROUP):
                row = (32 * ((b >> 1) & 1) + (b >> 2)) * 8 + (b & 1) * 4 + k * 2 + upper
                vectors.append(recv[pl.ds(row, 8, stride=32), :])
            moved = exchange(snake_sublanes(snake_chunks(vectors)))
            for b in range(GROUP):
                ref[upper * GROUP + b] = moved[b]
        return carry

    lax.fori_loop(0, 2, body, 0)


def shape(rows):
    return jax.ShapeDtypeStruct((rows, LANES), jnp.float32)


VMEM = pl.BlockSpec(memory_space=pltpu.VMEM)
SMEM = pl.BlockSpec(memory_space=pltpu.SMEM)


def per_device(pressure, source, facies, mobility_table):
    flat = [x.reshape(ROWS, 32, LANES) for x in (pressure, source, facies)]
    tiles = pl.BlockSpec((ROWS, 8, LANES), lambda g: (0, g, 0))
    sent = pl.pallas_call(
        pack_kernel,
        out_shape=shape(3072),
        grid=(4,),
        in_specs=[SMEM, tiles, tiles, tiles],
        out_specs=pl.BlockSpec((768, LANES), lambda g: (g, 0)),
        name="pack",
    )(mobility_table, *flat)
    recv = lax.all_to_all(sent.reshape(256, FIELDS, 4, LANES), AXES, 0, 0, tiled=True).reshape(3072, LANES)
    lower, upper = pl.pallas_call(
        halves_kernel,
        out_shape=(shape(1536), shape(1536)),
        in_specs=[VMEM],
        out_specs=(VMEM, VMEM),
        name="halves",
    )(recv)
    chain = [device_of(t) for t in range(256)]
    right_halo = lax.ppermute(lower, AXES, list(zip(chain[1:], chain[:-1])))
    left_halo = lax.ppermute(upper, AXES, list(zip(chain[:-1], chain[1:])))

    def cells(count):
        return pltpu.VMEM((count,) + SLAB, jnp.float32)

    result = pl.pallas_call(
        work_kernel,
        out_shape=shape(2048),
        in_specs=[VMEM, VMEM, VMEM],
        out_specs=VMEM,
        scratch_shapes=[
            cells(ROWS + 2),
            cells(ROWS + 2),
            cells(ROWS + 2),
            cells(ROWS + 2),
            cells(ROWS),
            cells(ROWS),
            cells(ROWS),
            cells(ROWS + 1),
        ],
        name="work",
    )(recv, left_halo, right_halo)
    back = lax.all_to_all(result.reshape(256, 8, LANES), AXES, 0, 0, tiled=True).reshape(2048, LANES)
    outs = pl.pallas_call(
        unpack_kernel,
        out_shape=(jax.ShapeDtypeStruct((ROWS, 32, LANES), jnp.float32),) * 2,
        grid=(4,),
        in_specs=[pl.BlockSpec((512, LANES), lambda g: (g, 0))],
        out_specs=(tiles, tiles),
        name="unpack",
    )(back)
    return tuple(x.reshape(pressure.shape) for x in outs)


def solution(mesh):
    spec = P("strike", "cross", None)
    return jax.shard_map(
        per_device,
        mesh=mesh,
        in_specs=(spec, spec, spec, P()),
        out_specs=(spec, spec),
        check_vma=False,
    )
```

```python
import math

import jax
import jax.numpy as jnp
from jax import lax
from jax.experimental import pallas as pl
from jax.experimental.pallas import tpu as pltpu
from jax.sharding import PartitionSpec as P

ND = 1024
CLASSES = 8
DEFECT = 2
SWEEPS = 3

STORE = 0.5
LOW = 0.05
HIGH = 1.95

LANES = 128
BLOCKS = 32
ROWS = ND // BLOCKS
GROUP = 16
AXES = ("cross", "strike")
FIELDS = 3
UNROLL = 4
HALF = 2 * FIELDS


def chebyshev_weights(count):
    middle = 0.5 * (LOW + HIGH)
    half = 0.5 * (HIGH - LOW)
    return [
        1.0 / (middle + half * math.cos(math.pi * (2 * j + 1) / (2 * count))) for j in range(count)
    ]


def device_of(chunk):
    row, q = divmod(chunk, 8)
    z, s = divmod(row, 8)
    if s % 2:
        q = 7 - q
    place = s if s < 4 else 11 - s
    return 64 * z + 4 * place + 32 * (q % 2) + q // 2


def exchange(vectors, keep=range(GROUP)):
    block = lax.broadcasted_iota(jnp.int32, vectors[0].shape, 1) // 8
    vectors = [pltpu.roll(vectors[k], 8 * k, 1) if k else vectors[k] for k in range(GROUP)]
    vectors = [vectors[-k % GROUP] for k in range(GROUP)]
    for step in (1, 2, 4):
        here = (block & step) != 0
        vectors = [jnp.where(here, vectors[(k - step) % GROUP], vectors[k]) for k in range(GROUP)]
    here = block >= 8
    done = {}
    for b in keep:
        moved = jnp.where(here, vectors[(b - 8) % GROUP], vectors[b])
        done[b] = pltpu.roll(moved, LANES - 8 * b, 1) if b else moved
    return done


def snake_sublanes(vectors):
    row = lax.broadcasted_iota(jnp.int32, (8, LANES), 0)
    order = jnp.where(row < 4, row, 11 - row)
    return [jnp.take_along_axis(v, order, axis=0) for v in vectors]


def snake_chunks(vectors):
    row = lax.broadcasted_iota(jnp.int32, (8, LANES), 0)
    odd = ((row & 1) ^ (row >> 2)) != 0
    return [
        jnp.where(odd, vectors[GROUP - 2 - (k & -2) + (k & 1)], vectors[k]) for k in range(GROUP)
    ]


def pack_kernel(table, pressure, source, facies, out):
    def lookup(codes):
        base = jnp.zeros(codes.shape, jnp.float32)
        for code in range(CLASSES):
            base = jnp.where(codes == code, table[code], base)
        return base

    def body(upper, carry):
        def read(ref):
            return [ref[upper * GROUP + b] for b in range(GROUP)]

        fields = (read(pressure), [lookup(c) for c in read(facies)], read(source))
        for k, vectors in enumerate(fields):
            moved = snake_chunks(exchange(snake_sublanes(vectors)))
            for b in range(GROUP):
                row = (32 * ((b >> 1) & 1) + (b >> 2)) * 2 * HALF + (b & 1) * HALF + k * 2 + upper
                out[pl.ds(row, 8, stride=8 * HALF), :] = moved[b]
        return carry

    lax.fori_loop(0, 2, body, 0, unroll=2)


def halves_kernel(recv, lower, upper):
    def body(g, carry):
        for w in range(HALF):
            rows = pl.ds(w * 256 + g * 8, 8)
            lower[rows, :] = recv[pl.ds(g * 8 * 2 * HALF + w, 8, stride=2 * HALF), :]
            upper[rows, :] = recv[pl.ds(g * 8 * 2 * HALF + HALF + w, 8, stride=2 * HALF), :]
        return carry

    lax.fori_loop(0, 32, body, 0)


SLAB = (8, 8, LANES)


def roll_lanes(x, shift):
    return pltpu.roll(x.reshape(64, LANES), shift % LANES, 1).reshape(x.shape)


def shift_blocks(x, shift):
    lane = lax.broadcasted_iota(jnp.int32, SLAB, 2)
    if abs(shift) >= 8:
        lanes = shift * 4
        keep = (lane >= lanes) if shift > 0 else (lane < LANES + lanes)
        return jnp.where(keep, roll_lanes(x, lanes), 0.0)
    sub = lax.broadcasted_iota(jnp.int32, SLAB, 1)
    near = jnp.stack([pltpu.roll(x[c], shift % 8, 0) for c in range(8)])
    if shift > 0:
        far = jnp.where(lane >= 32, roll_lanes(near, 32), 0.0)
        return jnp.where(sub >= shift, near, far)
    far = jnp.where(lane < 96, roll_lanes(near, -32), 0.0)
    return jnp.where(sub < 8 + shift, near, far)


def column_sum(x):
    total = jnp.broadcast_to(jnp.sum(x, axis=1, keepdims=True), SLAB)
    total = total + roll_lanes(total, 32)
    return total + roll_lanes(total, 64)


def roll_sublanes(x, shift):
    return jnp.stack([pltpu.roll(x[c], shift % 8, 0) for c in range(8)])


def work_kernel(own, left_halo, right_halo, out, p, m, base, source, resid, rho, part, power):
    omega = chebyshev_weights(SWEEPS)
    fields = (p, base, source)

    def unpack(g, carry):
        upper, c = g // 8, g % 8
        for k in range(FIELDS):
            vectors = []
            w = k * 2 + upper
            for tile in range(4):
                block = c * 32 + tile * 8
                vectors.append(left_halo[pl.ds(w * 256 + block, 8), :])
                vectors.append(own[pl.ds(block * 2 * HALF + w, 8, stride=2 * HALF), :])
                vectors.append(own[pl.ds(block * 2 * HALF + HALF + w, 8, stride=2 * HALF), :])
                vectors.append(right_halo[pl.ds(w * 256 + block, 8), :])
            moved = exchange(vectors)
            for b in range(GROUP):
                fields[k][upper * GROUP + b + 1, c] = moved[b]
        return carry

    lax.fori_loop(0, 16, unpack, 0, unroll=2)

    lane = lax.broadcasted_iota(jnp.int32, SLAB, 2)
    sub = lax.broadcasted_iota(jnp.int32, SLAB, 1)

    zeros = tuple(jnp.zeros((8, LANES), jnp.float32) for _ in range(8))

    def mobility(i, c, field):
        value = base[i + 1, c] * (0.5 + 0.25 * jnp.tanh(field))
        m[i + 1, c] = value
        return value

    def start(i, acc):
        return tuple(acc[c] + mobility(i, c, p[i + 1, c]) for c in range(8))

    total = jnp.stack(lax.fori_loop(0, ROWS, start, zeros, unroll=UNROLL))

    for step in range(DEFECT):
        for ref in (p, m):
            ref[0] = shift_blocks(ref[ROWS], 1)
            ref[ROWS + 1] = shift_blocks(ref[1], -1)

        mref = column_sum(total) * (2.0 / ND)
        inside = mref > 0.0
        safe = jnp.where(inside, mref, 1.0)
        half = 0.5 * (4.0 + STORE / safe)
        ratio = 1.0 / (1.0 + half + jnp.sqrt(half * (half + 2.0)))
        gain = ratio / ((1.0 - ratio * ratio) * safe)
        inner = gain * mref
        gain = jnp.where(inside, gain, 0.0)

        def powers(i, value):
            power[i] = value
            return value * ratio

        block_ratio = lax.fori_loop(0, ROWS, powers, jnp.ones(SLAB, jnp.float32), unroll=2)
        power[ROWS] = block_ratio
        squares = [block_ratio]
        for _ in range(5):
            squares.append(squares[-1] * squares[-1])
        whole = squares[5]
        reflect = 1.0 / (1.0 - whole * whole)
        below_sub = jnp.ones(SLAB, jnp.float32)
        above_sub = jnp.ones(SLAB, jnp.float32)
        for bit in range(3):
            on = ((sub >> bit) & 1) != 0
            below_sub = jnp.where(on, below_sub * squares[bit], below_sub)
            above_sub = jnp.where(on, above_sub, above_sub * squares[bit])
        from_left, from_right = below_sub, above_sub
        for bit in range(2):
            on = ((lane >> (5 + bit)) & 1) != 0
            from_left = jnp.where(on, from_left * squares[3 + bit], from_left)
            from_right = jnp.where(on, from_right, from_right * squares[3 + bit])

        def spread(x, kept):
            x = jnp.where(kept, x, 0.0)
            x = x + roll_lanes(x, 32)
            return x + roll_lanes(x, 64)

        def carries(ends, heads):
            for bit in range(3):
                s = 1 << bit
                ends = ends + squares[bit] * jnp.where(sub >= s, roll_sublanes(ends, s), 0.0)
                heads = heads + squares[bit] * jnp.where(sub < 8 - s, roll_sublanes(heads, -s), 0.0)
            end = jnp.broadcast_to(ends[:, 7:8], SLAB)
            head = jnp.broadcast_to(heads[:, 0:1], SLAB)
            before, after = shift_blocks(end, 8), shift_blocks(head, -8)
            before = before + squares[3] * shift_blocks(before, 8)
            after = after + squares[3] * shift_blocks(after, -8)
            before = before + squares[4] * shift_blocks(before, 16)
            after = after + squares[4] * shift_blocks(after, -16)
            a = spread(head + squares[3] * after, lane < 32)
            b = spread(end + squares[3] * before, lane >= 96)
            before = jnp.where(sub > 0, roll_sublanes(ends, 1), 0.0) + below_sub * before
            after = jnp.where(sub < 7, roll_sublanes(heads, -1), 0.0) + above_sub * after
            before = before + from_left * ((a + whole * b) * reflect)
            after = after + from_right * ((b + whole * a) * reflect)
            return before, after

        first_gain = omega[0] * gain

        def along(x, shift):
            return pltpu.roll(x, shift % LANES, 1)

        def form(i, carry):
            y, other, above = carry
            here = [p[i + 1, c] for c in range(8)]
            mob = [m[i + 1, c] for c in range(8)]
            new_y, new_other, new_above = [], [], []
            left = mob[0] * -here[0]
            for c in range(8):
                below = (mob[c] + m[i + 2, c]) * (here[c] - p[i + 2, c])
                if c < 7:
                    right = (mob[c] + mob[c + 1]) * (here[c] - here[c + 1])
                else:
                    right = mob[c] * here[c]
                strike = (mob[c] + along(mob[c], -1)) * (here[c] - along(here[c], -1))
                flow = (below - above[c]) + (right - left) + (strike - along(strike, 1))
                left = right
                result = (source[i + 1, c] - STORE * here[c]) - flow
                if step + 1 == DEFECT:
                    resid[i, c] = result
                value = first_gain[c] * result
                rho[i, c] = value
                value_y = value + ratio[c] * y[c]
                part[i, c] = value_y
                new_y.append(value_y)
                new_other.append(other[c] + power[i, c] * value)
                new_above.append(below)
            return tuple(new_y), tuple(new_other), tuple(new_above)

        first = tuple((m[0, c] + m[1, c]) * (p[0, c] - p[1, c]) for c in range(8))
        ends, heads, _ = lax.fori_loop(0, ROWS, form, (zeros, zeros, first), unroll=UNROLL)
        for sweep in range(SWEEPS):
            before, after = carries(jnp.stack(ends), jnp.stack(heads))
            down = sweep % 2 == 0
            entering, stored = (after, before) if down else (before, after)
            entering = tuple(entering[c] for c in range(8))

            def solved(n, c, running):
                i = ROWS - 1 - n if down else n
                value = rho[i, c]
                opposite = ratio[c] * running
                v = (part[i, c] + opposite) + power[ROWS - n, c] * stored[c]
                field = p[i + 1, c] + v
                p[i + 1, c] = field
                return value, value + opposite, v, field

            if sweep + 1 < SWEEPS:
                scaled = omega[sweep + 1] * inner
                keep = omega[sweep + 1] * (1.0 - omega[sweep]) / omega[sweep]

                def advance(n, carry):
                    running, x, other = carry
                    i = ROWS - 1 - n if down else n
                    new_running, new_x, new_other = [], [], []
                    values, vs = [], []

                    def finish(c):
                        near = along(vs[c], 1) + along(vs[c], -1)
                        if c:
                            near = near + vs[c - 1]
                        if c < 7:
                            near = near + vs[c + 1]
                        value = scaled[c] * near
                        if keep:
                            value = keep * values[c] + value
                        rho[i, c] = value
                        value_x = value + ratio[c] * x[c]
                        part[i, c] = value_x
                        new_x.append(value_x)
                        new_other.append(other[c] + power[n, c] * value)

                    for c in range(8):
                        value, run, v, _ = solved(n, c, running[c])
                        values.append(value)
                        new_running.append(run)
                        vs.append(v)
                        if c:
                            finish(c - 1)
                    finish(7)
                    return tuple(new_running), tuple(new_x), tuple(new_other)

                _, x, other = lax.fori_loop(0, ROWS, advance, (entering, zeros, zeros), unroll=UNROLL)
                ends, heads = (other, x) if down else (x, other)
            elif step + 1 < DEFECT:

                def renew(n, carry):
                    running, acc = carry
                    i = ROWS - 1 - n if down else n
                    new_running, new_acc = [], []
                    for c in range(8):
                        _, run, _, field = solved(n, c, running[c])
                        new_running.append(run)
                        new_acc.append(acc[c] + mobility(i, c, field))
                    return tuple(new_running), tuple(new_acc)

                total = jnp.stack(lax.fori_loop(0, ROWS, renew, (entering, zeros), unroll=UNROLL)[1])
            else:

                def last(n, running):
                    return tuple(solved(n, c, running[c])[1] for c in range(8))

                lax.fori_loop(0, ROWS, last, entering, unroll=UNROLL)

    kept = tuple(4 * tile + s for tile in range(4) for s in (1, 2))

    def pack(g, carry):
        upper, c = g // 8, g % 8
        for k, (ref, offset) in enumerate(((p, 1), (resid, 0))):
            moved = exchange([ref[upper * GROUP + b + offset, c] for b in range(GROUP)], kept)
            for tile in range(4):
                for s in range(2):
                    row = (c * 32 + tile * 8) * 8 + s * 4 + k * 2 + upper
                    out[pl.ds(row, 8, stride=8), :] = moved[4 * tile + 1 + s]
        return carry

    lax.fori_loop(0, 16, pack, 0, unroll=2)


def unpack_kernel(recv, pressure, defect):
    def body(upper, carry):
        for k, ref in enumerate((pressure, defect)):
            vectors = []
            for b in range(GROUP):
                row = (32 * ((b >> 1) & 1) + (b >> 2)) * 8 + (b & 1) * 4 + k * 2 + upper
                vectors.append(recv[pl.ds(row, 8, stride=32), :])
            moved = exchange(snake_sublanes(snake_chunks(vectors)))
            for b in range(GROUP):
                ref[upper * GROUP + b] = moved[b]
        return carry

    lax.fori_loop(0, 2, body, 0, unroll=2)


def shape(rows):
    return jax.ShapeDtypeStruct((rows, LANES), jnp.float32)


VMEM = pl.BlockSpec(memory_space=pltpu.VMEM)
SMEM = pl.BlockSpec(memory_space=pltpu.SMEM)


def per_device(pressure, source, facies, mobility_table):
    flat = [x.reshape(ROWS, 32, LANES) for x in (pressure, source, facies)]
    tiles = pl.BlockSpec((ROWS, 8, LANES), lambda g: (0, g, 0))
    sent = pl.pallas_call(
        pack_kernel,
        out_shape=shape(3072),
        grid=(4,),
        in_specs=[SMEM, tiles, tiles, tiles],
        out_specs=pl.BlockSpec((768, LANES), lambda g: (g, 0)),
        name="pack",
    )(mobility_table, *flat)
    recv = lax.all_to_all(sent.reshape(256, FIELDS, 4, LANES), AXES, 0, 0, tiled=True).reshape(3072, LANES)
    lower, upper = pl.pallas_call(
        halves_kernel,
        out_shape=(shape(1536), shape(1536)),
        in_specs=[VMEM],
        out_specs=(VMEM, VMEM),
        name="halves",
    )(recv)
    chain = [device_of(t) for t in range(256)]
    right_halo = lax.ppermute(lower, AXES, list(zip(chain[1:], chain[:-1])))
    left_halo = lax.ppermute(upper, AXES, list(zip(chain[:-1], chain[1:])))

    def cells(count):
        return pltpu.VMEM((count,) + SLAB, jnp.float32)

    result = pl.pallas_call(
        work_kernel,
        out_shape=shape(2048),
        in_specs=[VMEM, VMEM, VMEM],
        out_specs=VMEM,
        scratch_shapes=[
            cells(ROWS + 2),
            cells(ROWS + 2),
            cells(ROWS + 2),
            cells(ROWS + 2),
            cells(ROWS),
            cells(ROWS),
            cells(ROWS),
            cells(ROWS + 1),
        ],
        name="work",
    )(recv, left_halo, right_halo)
    back = lax.all_to_all(result.reshape(256, 8, LANES), AXES, 0, 0, tiled=True).reshape(2048, LANES)
    outs = pl.pallas_call(
        unpack_kernel,
        out_shape=(jax.ShapeDtypeStruct((ROWS, 32, LANES), jnp.float32),) * 2,
        grid=(4,),
        in_specs=[pl.BlockSpec((512, LANES), lambda g: (g, 0))],
        out_specs=(tiles, tiles),
        name="unpack",
    )(back)
    return tuple(x.reshape(pressure.shape) for x in outs)


def solution(mesh):
    spec = P("strike", "cross", None)
    return jax.shard_map(
        per_device,
        mesh=mesh,
        in_specs=(spec, spec, spec, P()),
        out_specs=(spec, spec),
        check_vma=False,
    )
```

```python
import math

import jax
import jax.numpy as jnp
from jax import lax
from jax.experimental import pallas as pl
from jax.experimental.pallas import tpu as pltpu
from jax.sharding import PartitionSpec as P

ND = 1024
CLASSES = 8
DEFECT = 2
SWEEPS = 3

STORE = 0.5
LOW = 0.05
HIGH = 1.95

LANES = 128
BLOCKS = 32
ROWS = ND // BLOCKS
GROUP = 16
AXES = ("cross", "strike")
FIELDS = 3
UNROLL = 4
HALF = 2 * FIELDS


def chebyshev_weights(count):
    middle = 0.5 * (LOW + HIGH)
    half = 0.5 * (HIGH - LOW)
    return [
        1.0 / (middle + half * math.cos(math.pi * (2 * j + 1) / (2 * count))) for j in range(count)
    ]


def device_of(chunk):
    row, q = divmod(chunk, 8)
    z, s = divmod(row, 8)
    if s % 2:
        q = 7 - q
    place = s if s < 4 else 11 - s
    return 64 * z + 4 * place + 32 * (q % 2) + q // 2


def exchange(vectors, keep=range(GROUP)):
    block = lax.broadcasted_iota(jnp.int32, vectors[0].shape, 1) // 8
    vectors = [pltpu.roll(vectors[k], 8 * k, 1) if k else vectors[k] for k in range(GROUP)]
    vectors = [vectors[-k % GROUP] for k in range(GROUP)]
    for step in (1, 2, 4):
        here = (block & step) != 0
        vectors = [jnp.where(here, vectors[(k - step) % GROUP], vectors[k]) for k in range(GROUP)]
    here = block >= 8
    done = {}
    for b in keep:
        moved = jnp.where(here, vectors[(b - 8) % GROUP], vectors[b])
        done[b] = pltpu.roll(moved, LANES - 8 * b, 1) if b else moved
    return done


def snake_sublanes(vectors):
    row = lax.broadcasted_iota(jnp.int32, (8, LANES), 0)
    order = jnp.where(row < 4, row, 11 - row)
    return [jnp.take_along_axis(v, order, axis=0) for v in vectors]


def snake_chunks(vectors):
    row = lax.broadcasted_iota(jnp.int32, (8, LANES), 0)
    odd = ((row & 1) ^ (row >> 2)) != 0
    return [
        jnp.where(odd, vectors[GROUP - 2 - (k & -2) + (k & 1)], vectors[k]) for k in range(GROUP)
    ]


def pack_kernel(table, pressure, source, facies, out):
    def lookup(codes):
        base = jnp.zeros(codes.shape, jnp.float32)
        for code in range(CLASSES):
            base = jnp.where(codes == code, table[code], base)
        return base

    def body(upper, carry):
        def read(ref):
            return [ref[upper * GROUP + b] for b in range(GROUP)]

        fields = (read(pressure), [lookup(c) for c in read(facies)], read(source))
        for k, vectors in enumerate(fields):
            moved = snake_chunks(exchange(snake_sublanes(vectors)))
            for b in range(GROUP):
                row = (32 * ((b >> 1) & 1) + (b >> 2)) * 2 * HALF + (b & 1) * HALF + k * 2 + upper
                out[pl.ds(row, 8, stride=8 * HALF), :] = moved[b]
        return carry

    lax.fori_loop(0, 2, body, 0, unroll=2)


def cell_index():
    return lax.broadcasted_iota(jnp.int32, (8, LANES), 1) % 8


def squeeze(four, tail):
    cell = cell_index()
    free = cell < 2 if tail else cell >= 6
    sign = -1 if tail else 1
    shifts = (2, 4, 6) if tail else (6, 4, 2)
    return [jnp.where(free, pltpu.roll(four[3], sign * n % LANES, 1), v) for v, n in zip(four, shifts)]


def stretch(three, tail):
    cell = cell_index()
    if tail:
        a, b, c = (pltpu.roll(v, n, 1) for v, n in zip(three, (2, 4, 6)))
        return list(three) + [jnp.where(cell >= 6, c, jnp.where(cell >= 4, b, a))]
    a, b, c = (pltpu.roll(v, LANES - n, 1) for v, n in zip(three, (6, 4, 2)))
    return list(three) + [jnp.where(cell < 2, a, jnp.where(cell < 4, b, c))]


def halves_kernel(recv, lower, upper, whole, first, second, sems):
    def arrival(c):
        span = pl.ds(c * 64 * HALF, 64 * HALF)
        return pltpu.make_async_copy(recv.at[span], whole.at[span], sems.at[2, c])

    def departure(c, side):
        span = pl.ds(c * 24 * HALF, 24 * HALF)
        return pltpu.make_async_copy((first, second)[side].at[span], (lower, upper)[side].at[span], sems.at[side, c])

    for c in range(8):
        arrival(c).start()

    def body(c, carry):
        arrival(c).wait()
        for side, ref in enumerate((first, second)):
            for w in range(HALF):
                four = [
                    whole[pl.ds((c * 32 + tile * 8) * 2 * HALF + side * HALF + w, 8, stride=2 * HALF), :]
                    for tile in range(4)
                ]
                for n, vector in enumerate(squeeze(four, side == 1)):
                    ref[pl.ds((c * HALF + w) * 24 + n * 8, 8), :] = vector
            departure(c, side).start()
        return carry

    lax.fori_loop(0, 8, body, 0)
    for c in range(8):
        for side in range(2):
            departure(c, side).wait()


SLAB = (8, 8, LANES)


def roll_lanes(x, shift):
    return pltpu.roll(x.reshape(64, LANES), shift % LANES, 1).reshape(x.shape)


def shift_blocks(x, shift):
    lane = lax.broadcasted_iota(jnp.int32, SLAB, 2)
    if abs(shift) >= 8:
        lanes = shift * 4
        keep = (lane >= lanes) if shift > 0 else (lane < LANES + lanes)
        return jnp.where(keep, roll_lanes(x, lanes), 0.0)
    sub = lax.broadcasted_iota(jnp.int32, SLAB, 1)
    near = jnp.stack([pltpu.roll(x[c], shift % 8, 0) for c in range(8)])
    if shift > 0:
        far = jnp.where(lane >= 32, roll_lanes(near, 32), 0.0)
        return jnp.where(sub >= shift, near, far)
    far = jnp.where(lane < 96, roll_lanes(near, -32), 0.0)
    return jnp.where(sub < 8 + shift, near, far)


def column_sum(x):
    total = jnp.broadcast_to(jnp.sum(x, axis=1, keepdims=True), SLAB)
    total = total + roll_lanes(total, 32)
    return total + roll_lanes(total, 64)


def roll_sublanes(x, shift):
    return jnp.stack([pltpu.roll(x[c], shift % 8, 0) for c in range(8)])


def work_kernel(
    own_in, left_in, right_in, out, p, m, base, source, resid, rho, part, power, own, left, right, sent, sems
):
    omega = chebyshev_weights(SWEEPS)
    fields = (p, base, source)

    def arrivals(c):
        for k, (there, here, rows) in enumerate(
            ((own_in, own, 64 * HALF), (left_in, left, 24 * HALF), (right_in, right, 24 * HALF))
        ):
            span = pl.ds(c * rows, rows)
            yield pltpu.make_async_copy(there.at[span], here.at[span], sems.at[k, c])

    for c in range(8):
        for copy in arrivals(c):
            copy.start()

    def unpack(c, carry):
        for copy in arrivals(c):
            copy.wait()
        for upper in range(2):
            for k in range(FIELDS):
                vectors = []
                w = k * 2 + upper
                first = (c * HALF + w) * 24
                before = stretch([left[pl.ds(first + n * 8, 8), :] for n in range(3)], True)
                after = stretch([right[pl.ds(first + n * 8, 8), :] for n in range(3)], False)
                for tile in range(4):
                    block = c * 32 + tile * 8
                    vectors.append(before[tile])
                    vectors.append(own[pl.ds(block * 2 * HALF + w, 8, stride=2 * HALF), :])
                    vectors.append(own[pl.ds(block * 2 * HALF + HALF + w, 8, stride=2 * HALF), :])
                    vectors.append(after[tile])
                moved = exchange(vectors)
                for b in range(GROUP):
                    fields[k][upper * GROUP + b + 1, c] = moved[b]
        return carry

    lax.fori_loop(0, 8, unpack, 0)

    lane = lax.broadcasted_iota(jnp.int32, SLAB, 2)
    sub = lax.broadcasted_iota(jnp.int32, SLAB, 1)

    zeros = tuple(jnp.zeros((8, LANES), jnp.float32) for _ in range(8))

    def mobility(i, c, field):
        value = base[i + 1, c] * (0.5 + 0.25 * jnp.tanh(field))
        m[i + 1, c] = value
        return value

    def start(i, acc):
        return tuple(acc[c] + mobility(i, c, p[i + 1, c]) for c in range(8))

    total = jnp.stack(lax.fori_loop(0, ROWS, start, zeros, unroll=UNROLL))

    for step in range(DEFECT):
        for ref in (p, m):
            ref[0] = shift_blocks(ref[ROWS], 1)
            ref[ROWS + 1] = shift_blocks(ref[1], -1)

        mref = column_sum(total) * (2.0 / ND)
        inside = mref > 0.0
        safe = jnp.where(inside, mref, 1.0)
        half = 0.5 * (4.0 + STORE / safe)
        ratio = 1.0 / (1.0 + half + jnp.sqrt(half * (half + 2.0)))
        gain = ratio / ((1.0 - ratio * ratio) * safe)
        inner = gain * mref
        gain = jnp.where(inside, gain, 0.0)

        def powers(i, value):
            power[i] = value
            return value * ratio

        block_ratio = lax.fori_loop(0, ROWS, powers, jnp.ones(SLAB, jnp.float32), unroll=2)
        power[ROWS] = block_ratio
        squares = [block_ratio]
        for _ in range(5):
            squares.append(squares[-1] * squares[-1])
        whole = squares[5]
        reflect = 1.0 / (1.0 - whole * whole)
        below_sub = jnp.ones(SLAB, jnp.float32)
        above_sub = jnp.ones(SLAB, jnp.float32)
        for bit in range(3):
            on = ((sub >> bit) & 1) != 0
            below_sub = jnp.where(on, below_sub * squares[bit], below_sub)
            above_sub = jnp.where(on, above_sub, above_sub * squares[bit])
        from_left, from_right = below_sub, above_sub
        for bit in range(2):
            on = ((lane >> (5 + bit)) & 1) != 0
            from_left = jnp.where(on, from_left * squares[3 + bit], from_left)
            from_right = jnp.where(on, from_right, from_right * squares[3 + bit])

        def spread(x, kept):
            x = jnp.where(kept, x, 0.0)
            x = x + roll_lanes(x, 32)
            return x + roll_lanes(x, 64)

        def carries(ends, heads):
            for bit in range(3):
                s = 1 << bit
                ends = ends + squares[bit] * jnp.where(sub >= s, roll_sublanes(ends, s), 0.0)
                heads = heads + squares[bit] * jnp.where(sub < 8 - s, roll_sublanes(heads, -s), 0.0)
            end = jnp.broadcast_to(ends[:, 7:8], SLAB)
            head = jnp.broadcast_to(heads[:, 0:1], SLAB)
            before, after = shift_blocks(end, 8), shift_blocks(head, -8)
            before = before + squares[3] * shift_blocks(before, 8)
            after = after + squares[3] * shift_blocks(after, -8)
            before = before + squares[4] * shift_blocks(before, 16)
            after = after + squares[4] * shift_blocks(after, -16)
            a = spread(head + squares[3] * after, lane < 32)
            b = spread(end + squares[3] * before, lane >= 96)
            before = jnp.where(sub > 0, roll_sublanes(ends, 1), 0.0) + below_sub * before
            after = jnp.where(sub < 7, roll_sublanes(heads, -1), 0.0) + above_sub * after
            before = before + from_left * ((a + whole * b) * reflect)
            after = after + from_right * ((b + whole * a) * reflect)
            return before, after

        first_gain = omega[0] * gain

        def along(x, shift):
            return pltpu.roll(x, shift % LANES, 1)

        def form(i, carry):
            y, other, above = carry
            here = [p[i + 1, c] for c in range(8)]
            mob = [m[i + 1, c] for c in range(8)]
            new_y, new_other, new_above = [], [], []
            left = mob[0] * -here[0]
            for c in range(8):
                below = (mob[c] + m[i + 2, c]) * (here[c] - p[i + 2, c])
                if c < 7:
                    right = (mob[c] + mob[c + 1]) * (here[c] - here[c + 1])
                else:
                    right = mob[c] * here[c]
                strike = (mob[c] + along(mob[c], -1)) * (here[c] - along(here[c], -1))
                flow = (below - above[c]) + (right - left) + (strike - along(strike, 1))
                left = right
                result = (source[i + 1, c] - STORE * here[c]) - flow
                if step + 1 == DEFECT:
                    resid[i, c] = result
                value = first_gain[c] * result
                rho[i, c] = value
                value_y = value + ratio[c] * y[c]
                part[i, c] = value_y
                new_y.append(value_y)
                new_other.append(other[c] + power[i, c] * value)
                new_above.append(below)
            return tuple(new_y), tuple(new_other), tuple(new_above)

        first = tuple((m[0, c] + m[1, c]) * (p[0, c] - p[1, c]) for c in range(8))
        ends, heads, _ = lax.fori_loop(0, ROWS, form, (zeros, zeros, first), unroll=UNROLL)
        for sweep in range(SWEEPS):
            before, after = carries(jnp.stack(ends), jnp.stack(heads))
            down = sweep % 2 == 0
            entering, stored = (after, before) if down else (before, after)
            entering = tuple(entering[c] for c in range(8))

            def solved(n, c, running):
                i = ROWS - 1 - n if down else n
                value = rho[i, c]
                opposite = ratio[c] * running
                v = (part[i, c] + opposite) + power[ROWS - n, c] * stored[c]
                field = p[i + 1, c] + v
                p[i + 1, c] = field
                return value, value + opposite, v, field

            if sweep + 1 < SWEEPS:
                scaled = omega[sweep + 1] * inner
                keep = omega[sweep + 1] * (1.0 - omega[sweep]) / omega[sweep]

                def advance(n, carry):
                    running, x, other = carry
                    i = ROWS - 1 - n if down else n
                    new_running, new_x, new_other = [], [], []
                    values, vs = [], []

                    def finish(c):
                        near = along(vs[c], 1) + along(vs[c], -1)
                        if c:
                            near = near + vs[c - 1]
                        if c < 7:
                            near = near + vs[c + 1]
                        value = scaled[c] * near
                        if keep:
                            value = keep * values[c] + value
                        rho[i, c] = value
                        value_x = value + ratio[c] * x[c]
                        part[i, c] = value_x
                        new_x.append(value_x)
                        new_other.append(other[c] + power[n, c] * value)

                    for c in range(8):
                        value, run, v, _ = solved(n, c, running[c])
                        values.append(value)
                        new_running.append(run)
                        vs.append(v)
                        if c:
                            finish(c - 1)
                    finish(7)
                    return tuple(new_running), tuple(new_x), tuple(new_other)

                _, x, other = lax.fori_loop(0, ROWS, advance, (entering, zeros, zeros), unroll=UNROLL)
                ends, heads = (other, x) if down else (x, other)
            elif step + 1 < DEFECT:

                def renew(n, carry):
                    running, acc = carry
                    i = ROWS - 1 - n if down else n
                    new_running, new_acc = [], []
                    for c in range(8):
                        _, run, _, field = solved(n, c, running[c])
                        new_running.append(run)
                        new_acc.append(acc[c] + mobility(i, c, field))
                    return tuple(new_running), tuple(new_acc)

                total = jnp.stack(lax.fori_loop(0, ROWS, renew, (entering, zeros), unroll=UNROLL)[1])
            else:

                def last(n, running):
                    return tuple(solved(n, c, running[c])[1] for c in range(8))

                lax.fori_loop(0, ROWS, last, entering, unroll=UNROLL)

    kept = tuple(4 * tile + s for tile in range(4) for s in (1, 2))

    def departure(c):
        span = pl.ds(c * 256, 256)
        return pltpu.make_async_copy(sent.at[span], out.at[span], sems.at[3, c])

    def pack(c, carry):
        for upper in range(2):
            for k, (ref, offset) in enumerate(((p, 1), (resid, 0))):
                moved = exchange([ref[upper * GROUP + b + offset, c] for b in range(GROUP)], kept)
                for tile in range(4):
                    for s in range(2):
                        row = (c * 32 + tile * 8) * 8 + s * 4 + k * 2 + upper
                        sent[pl.ds(row, 8, stride=8), :] = moved[4 * tile + 1 + s]
        departure(c).start()
        return carry

    lax.fori_loop(0, 8, pack, 0)
    for c in range(8):
        departure(c).wait()


def unpack_kernel(recv, pressure, defect):
    def body(upper, carry):
        for k, ref in enumerate((pressure, defect)):
            vectors = []
            for b in range(GROUP):
                row = (32 * ((b >> 1) & 1) + (b >> 2)) * 8 + (b & 1) * 4 + k * 2 + upper
                vectors.append(recv[pl.ds(row, 8, stride=32), :])
            moved = exchange(snake_sublanes(snake_chunks(vectors)))
            for b in range(GROUP):
                ref[upper * GROUP + b] = moved[b]
        return carry

    lax.fori_loop(0, 2, body, 0, unroll=2)


def shape(rows):
    return jax.ShapeDtypeStruct((rows, LANES), jnp.float32)


ANY = pl.BlockSpec(memory_space=pl.ANY)
VMEM = pl.BlockSpec(memory_space=pltpu.VMEM)
SMEM = pl.BlockSpec(memory_space=pltpu.SMEM)


def per_device(pressure, source, facies, mobility_table):
    flat = [x.reshape(ROWS, 32, LANES) for x in (pressure, source, facies)]
    tiles = pl.BlockSpec((ROWS, 8, LANES), lambda g: (0, g, 0))
    sent = pl.pallas_call(
        pack_kernel,
        out_shape=shape(3072),
        grid=(4,),
        in_specs=[SMEM, tiles, tiles, tiles],
        out_specs=pl.BlockSpec((768, LANES), lambda g: (g, 0)),
        name="pack",
    )(mobility_table, *flat)
    recv = lax.all_to_all(sent.reshape(256, FIELDS, 4, LANES), AXES, 0, 0, tiled=True).reshape(3072, LANES)
    lower, upper = pl.pallas_call(
        halves_kernel,
        out_shape=(shape(1152), shape(1152)),
        in_specs=[ANY],
        out_specs=(ANY, ANY),
        scratch_shapes=[
            pltpu.VMEM((3072, LANES), jnp.float32),
            pltpu.VMEM((1152, LANES), jnp.float32),
            pltpu.VMEM((1152, LANES), jnp.float32),
            pltpu.SemaphoreType.DMA((3, 8)),
        ],
        name="halves",
    )(recv)
    chain = [device_of(t) for t in range(256)]
    right_halo = lax.ppermute(lower, AXES, list(zip(chain[1:], chain[:-1])))
    left_halo = lax.ppermute(upper, AXES, list(zip(chain[:-1], chain[1:])))

    def cells(count):
        return pltpu.VMEM((count,) + SLAB, jnp.float32)

    result = pl.pallas_call(
        work_kernel,
        out_shape=shape(2048),
        in_specs=[ANY, ANY, ANY],
        out_specs=ANY,
        scratch_shapes=[
            cells(ROWS + 2),
            cells(ROWS + 2),
            cells(ROWS + 2),
            cells(ROWS + 2),
            cells(ROWS),
            cells(ROWS),
            cells(ROWS),
            cells(ROWS + 1),
            pltpu.VMEM((3072, LANES), jnp.float32),
            pltpu.VMEM((1152, LANES), jnp.float32),
            pltpu.VMEM((1152, LANES), jnp.float32),
            pltpu.VMEM((2048, LANES), jnp.float32),
            pltpu.SemaphoreType.DMA((4, 8)),
        ],
        name="work",
    )(recv, left_halo, right_halo)
    back = lax.all_to_all(result.reshape(256, 8, LANES), AXES, 0, 0, tiled=True).reshape(2048, LANES)
    outs = pl.pallas_call(
        unpack_kernel,
        out_shape=(jax.ShapeDtypeStruct((ROWS, 32, LANES), jnp.float32),) * 2,
        grid=(4,),
        in_specs=[pl.BlockSpec((512, LANES), lambda g: (g, 0))],
        out_specs=(tiles, tiles),
        name="unpack",
    )(back)
    return tuple(x.reshape(pressure.shape) for x in outs)


def solution(mesh):
    spec = P("strike", "cross", None)
    return jax.shard_map(
        per_device,
        mesh=mesh,
        in_specs=(spec, spec, spec, P()),
        out_specs=(spec, spec),
        check_vma=False,
    )
```

```python
import math

import jax
import jax.numpy as jnp
from jax import lax
from jax.experimental import pallas as pl
from jax.experimental.pallas import tpu as pltpu
from jax.sharding import PartitionSpec as P

ND = 1024
CLASSES = 8
DEFECT = 2
SWEEPS = 3

STORE = 0.5
LOW = 0.05
HIGH = 1.95

LANES = 128
BLOCKS = 32
ROWS = ND // BLOCKS
GROUP = 16
AXES = ("cross", "strike")
FIELDS = 3
UNROLL = 4
HALF = 2 * FIELDS


def chebyshev_weights(count):
    middle = 0.5 * (LOW + HIGH)
    half = 0.5 * (HIGH - LOW)
    return [
        1.0 / (middle + half * math.cos(math.pi * (2 * j + 1) / (2 * count))) for j in range(count)
    ]


def device_of(chunk):
    row, q = divmod(chunk, 8)
    z, s = divmod(row, 8)
    if s % 2:
        q = 7 - q
    place = s if s < 4 else 11 - s
    return 64 * z + 4 * place + 32 * (q % 2) + q // 2


def exchange(vectors, keep=range(GROUP)):
    block = lax.broadcasted_iota(jnp.int32, vectors[0].shape, 1) // 8
    vectors = [pltpu.roll(vectors[k], 8 * k, 1) if k else vectors[k] for k in range(GROUP)]
    vectors = [vectors[-k % GROUP] for k in range(GROUP)]
    for step in (1, 2, 4):
        here = (block & step) != 0
        vectors = [jnp.where(here, vectors[(k - step) % GROUP], vectors[k]) for k in range(GROUP)]
    here = block >= 8
    done = {}
    for b in keep:
        moved = jnp.where(here, vectors[(b - 8) % GROUP], vectors[b])
        done[b] = pltpu.roll(moved, LANES - 8 * b, 1) if b else moved
    return done


def snake_sublanes(vectors):
    row = lax.broadcasted_iota(jnp.int32, (8, LANES), 0)
    order = jnp.where(row < 4, row, 11 - row)
    return [jnp.take_along_axis(v, order, axis=0) for v in vectors]


def snake_chunks(vectors):
    row = lax.broadcasted_iota(jnp.int32, (8, LANES), 0)
    odd = ((row & 1) ^ (row >> 2)) != 0
    return [
        jnp.where(odd, vectors[GROUP - 2 - (k & -2) + (k & 1)], vectors[k]) for k in range(GROUP)
    ]


def tile_span(g):
    return pl.ds(pl.multiple_of(g * 8, 8), 8)


def pack_kernel(table, pressure_in, source_in, facies_in, out, pressure, source, facies, sent, sems):
    def arrivals(g):
        pairs = ((pressure_in, pressure), (facies_in, facies), (source_in, source))
        for k, (there, here) in enumerate(pairs):
            yield pltpu.make_async_copy(there.at[:, tile_span(g)], here.at[:, tile_span(g)], sems.at[k, g])

    def departure(g):
        span = pl.ds(g * 128 * HALF, 128 * HALF)
        return pltpu.make_async_copy(sent.at[span], out.at[span], sems.at[3, g])

    def lookup(codes):
        base = jnp.zeros(codes.shape, jnp.float32)
        for code in range(CLASSES):
            base = jnp.where(codes == code, table[code], base)
        return base

    for g in range(4):
        for copy in arrivals(g):
            copy.start()

    def body(g, carry):
        for copy in arrivals(g):
            copy.wait()
        for upper in range(2):

            def read(ref):
                return [ref[upper * GROUP + b, tile_span(g), :] for b in range(GROUP)]

            fields = (read(pressure), [lookup(c) for c in read(facies)], read(source))
            for k, vectors in enumerate(fields):
                moved = snake_chunks(exchange(snake_sublanes(vectors)))
                for b in range(GROUP):
                    first = 64 * g + 32 * ((b >> 1) & 1) + (b >> 2)
                    row = first * 2 * HALF + (b & 1) * HALF + k * 2 + upper
                    sent[pl.ds(row, 8, stride=8 * HALF), :] = moved[b]
        departure(g).start()
        return carry

    lax.fori_loop(0, 4, body, 0)
    for g in range(4):
        departure(g).wait()


def cell_index():
    return lax.broadcasted_iota(jnp.int32, (8, LANES), 1) % 8


def squeeze(four, tail):
    cell = cell_index()
    free = cell < 2 if tail else cell >= 6
    sign = -1 if tail else 1
    shifts = (2, 4, 6) if tail else (6, 4, 2)
    return [jnp.where(free, pltpu.roll(four[3], sign * n % LANES, 1), v) for v, n in zip(four, shifts)]


def stretch(three, tail):
    cell = cell_index()
    if tail:
        a, b, c = (pltpu.roll(v, n, 1) for v, n in zip(three, (2, 4, 6)))
        return list(three) + [jnp.where(cell >= 6, c, jnp.where(cell >= 4, b, a))]
    a, b, c = (pltpu.roll(v, LANES - n, 1) for v, n in zip(three, (6, 4, 2)))
    return list(three) + [jnp.where(cell < 2, a, jnp.where(cell < 4, b, c))]


def halves_kernel(recv, lower, upper, whole, first, second, sems):
    def arrival(c):
        span = pl.ds(c * 64 * HALF, 64 * HALF)
        return pltpu.make_async_copy(recv.at[span], whole.at[span], sems.at[2, c])

    def departure(c, side):
        span = pl.ds(c * 24 * HALF, 24 * HALF)
        return pltpu.make_async_copy((first, second)[side].at[span], (lower, upper)[side].at[span], sems.at[side, c])

    for c in range(8):
        arrival(c).start()

    def body(c, carry):
        arrival(c).wait()
        for side, ref in enumerate((first, second)):
            for w in range(HALF):
                four = [
                    whole[pl.ds((c * 32 + tile * 8) * 2 * HALF + side * HALF + w, 8, stride=2 * HALF), :]
                    for tile in range(4)
                ]
                for n, vector in enumerate(squeeze(four, side == 1)):
                    ref[pl.ds((c * HALF + w) * 24 + n * 8, 8), :] = vector
            departure(c, side).start()
        return carry

    lax.fori_loop(0, 8, body, 0)
    for c in range(8):
        for side in range(2):
            departure(c, side).wait()


SLAB = (8, 8, LANES)


def roll_lanes(x, shift):
    return pltpu.roll(x.reshape(64, LANES), shift % LANES, 1).reshape(x.shape)


def shift_blocks(x, shift):
    lane = lax.broadcasted_iota(jnp.int32, SLAB, 2)
    if abs(shift) >= 8:
        lanes = shift * 4
        keep = (lane >= lanes) if shift > 0 else (lane < LANES + lanes)
        return jnp.where(keep, roll_lanes(x, lanes), 0.0)
    sub = lax.broadcasted_iota(jnp.int32, SLAB, 1)
    near = jnp.stack([pltpu.roll(x[c], shift % 8, 0) for c in range(8)])
    if shift > 0:
        far = jnp.where(lane >= 32, roll_lanes(near, 32), 0.0)
        return jnp.where(sub >= shift, near, far)
    far = jnp.where(lane < 96, roll_lanes(near, -32), 0.0)
    return jnp.where(sub < 8 + shift, near, far)


def column_sum(x):
    total = jnp.broadcast_to(jnp.sum(x, axis=1, keepdims=True), SLAB)
    total = total + roll_lanes(total, 32)
    return total + roll_lanes(total, 64)


def roll_sublanes(x, shift):
    return jnp.stack([pltpu.roll(x[c], shift % 8, 0) for c in range(8)])


def work_kernel(
    own_in, left_in, right_in, out, p, m, base, source, resid, rho, part, power, own, left, right, sent, sems
):
    omega = chebyshev_weights(SWEEPS)
    fields = (p, base, source)

    def arrivals(c):
        for k, (there, here, rows) in enumerate(
            ((own_in, own, 64 * HALF), (left_in, left, 24 * HALF), (right_in, right, 24 * HALF))
        ):
            span = pl.ds(c * rows, rows)
            yield pltpu.make_async_copy(there.at[span], here.at[span], sems.at[k, c])

    for c in range(8):
        for copy in arrivals(c):
            copy.start()

    def unpack(c, carry):
        for copy in arrivals(c):
            copy.wait()
        for upper in range(2):
            for k in range(FIELDS):
                vectors = []
                w = k * 2 + upper
                first = (c * HALF + w) * 24
                before = stretch([left[pl.ds(first + n * 8, 8), :] for n in range(3)], True)
                after = stretch([right[pl.ds(first + n * 8, 8), :] for n in range(3)], False)
                for tile in range(4):
                    block = c * 32 + tile * 8
                    vectors.append(before[tile])
                    vectors.append(own[pl.ds(block * 2 * HALF + w, 8, stride=2 * HALF), :])
                    vectors.append(own[pl.ds(block * 2 * HALF + HALF + w, 8, stride=2 * HALF), :])
                    vectors.append(after[tile])
                moved = exchange(vectors)
                for b in range(GROUP):
                    fields[k][upper * GROUP + b + 1, c] = moved[b]
        return carry

    lax.fori_loop(0, 8, unpack, 0)

    lane = lax.broadcasted_iota(jnp.int32, SLAB, 2)
    sub = lax.broadcasted_iota(jnp.int32, SLAB, 1)

    zeros = tuple(jnp.zeros((8, LANES), jnp.float32) for _ in range(8))

    def mobility(i, c, field):
        value = base[i + 1, c] * (0.5 + 0.25 * jnp.tanh(field))
        m[i + 1, c] = value
        return value

    def start(i, acc):
        return tuple(acc[c] + mobility(i, c, p[i + 1, c]) for c in range(8))

    total = jnp.stack(lax.fori_loop(0, ROWS, start, zeros, unroll=UNROLL))

    for step in range(DEFECT):
        for ref in (p, m):
            ref[0] = shift_blocks(ref[ROWS], 1)
            ref[ROWS + 1] = shift_blocks(ref[1], -1)

        mref = column_sum(total) * (2.0 / ND)
        inside = mref > 0.0
        safe = jnp.where(inside, mref, 1.0)
        half = 0.5 * (4.0 + STORE / safe)
        ratio = 1.0 / (1.0 + half + jnp.sqrt(half * (half + 2.0)))
        gain = ratio / ((1.0 - ratio * ratio) * safe)
        inner = gain * mref
        gain = jnp.where(inside, gain, 0.0)

        def powers(i, value):
            power[i] = value
            return value * ratio

        block_ratio = lax.fori_loop(0, ROWS, powers, jnp.ones(SLAB, jnp.float32), unroll=2)
        power[ROWS] = block_ratio
        squares = [block_ratio]
        for _ in range(5):
            squares.append(squares[-1] * squares[-1])
        whole = squares[5]
        reflect = 1.0 / (1.0 - whole * whole)
        below_sub = jnp.ones(SLAB, jnp.float32)
        above_sub = jnp.ones(SLAB, jnp.float32)
        for bit in range(3):
            on = ((sub >> bit) & 1) != 0
            below_sub = jnp.where(on, below_sub * squares[bit], below_sub)
            above_sub = jnp.where(on, above_sub, above_sub * squares[bit])
        from_left, from_right = below_sub, above_sub
        for bit in range(2):
            on = ((lane >> (5 + bit)) & 1) != 0
            from_left = jnp.where(on, from_left * squares[3 + bit], from_left)
            from_right = jnp.where(on, from_right, from_right * squares[3 + bit])

        def spread(x, kept):
            x = jnp.where(kept, x, 0.0)
            x = x + roll_lanes(x, 32)
            return x + roll_lanes(x, 64)

        def carries(ends, heads):
            for bit in range(3):
                s = 1 << bit
                ends = ends + squares[bit] * jnp.where(sub >= s, roll_sublanes(ends, s), 0.0)
                heads = heads + squares[bit] * jnp.where(sub < 8 - s, roll_sublanes(heads, -s), 0.0)
            end = jnp.broadcast_to(ends[:, 7:8], SLAB)
            head = jnp.broadcast_to(heads[:, 0:1], SLAB)
            before, after = shift_blocks(end, 8), shift_blocks(head, -8)
            before = before + squares[3] * shift_blocks(before, 8)
            after = after + squares[3] * shift_blocks(after, -8)
            before = before + squares[4] * shift_blocks(before, 16)
            after = after + squares[4] * shift_blocks(after, -16)
            a = spread(head + squares[3] * after, lane < 32)
            b = spread(end + squares[3] * before, lane >= 96)
            before = jnp.where(sub > 0, roll_sublanes(ends, 1), 0.0) + below_sub * before
            after = jnp.where(sub < 7, roll_sublanes(heads, -1), 0.0) + above_sub * after
            before = before + from_left * ((a + whole * b) * reflect)
            after = after + from_right * ((b + whole * a) * reflect)
            return before, after

        first_gain = omega[0] * gain

        def along(x, shift):
            return pltpu.roll(x, shift % LANES, 1)

        def form(i, carry):
            y, other, above = carry
            here = [p[i + 1, c] for c in range(8)]
            mob = [m[i + 1, c] for c in range(8)]
            new_y, new_other, new_above = [], [], []
            left = mob[0] * -here[0]
            for c in range(8):
                below = (mob[c] + m[i + 2, c]) * (here[c] - p[i + 2, c])
                if c < 7:
                    right = (mob[c] + mob[c + 1]) * (here[c] - here[c + 1])
                else:
                    right = mob[c] * here[c]
                strike = (mob[c] + along(mob[c], -1)) * (here[c] - along(here[c], -1))
                flow = (below - above[c]) + (right - left) + (strike - along(strike, 1))
                left = right
                result = (source[i + 1, c] - STORE * here[c]) - flow
                if step + 1 == DEFECT:
                    resid[i, c] = result
                value = first_gain[c] * result
                rho[i, c] = value
                value_y = value + ratio[c] * y[c]
                part[i, c] = value_y
                new_y.append(value_y)
                new_other.append(other[c] + power[i, c] * value)
                new_above.append(below)
            return tuple(new_y), tuple(new_other), tuple(new_above)

        first = tuple((m[0, c] + m[1, c]) * (p[0, c] - p[1, c]) for c in range(8))
        ends, heads, _ = lax.fori_loop(0, ROWS, form, (zeros, zeros, first), unroll=UNROLL)
        for sweep in range(SWEEPS):
            before, after = carries(jnp.stack(ends), jnp.stack(heads))
            down = sweep % 2 == 0
            entering, stored = (after, before) if down else (before, after)
            entering = tuple(entering[c] for c in range(8))

            def solved(n, c, running):
                i = ROWS - 1 - n if down else n
                value = rho[i, c]
                opposite = ratio[c] * running
                v = (part[i, c] + opposite) + power[ROWS - n, c] * stored[c]
                field = p[i + 1, c] + v
                p[i + 1, c] = field
                return value, value + opposite, v, field

            if sweep + 1 < SWEEPS:
                scaled = omega[sweep + 1] * inner
                keep = omega[sweep + 1] * (1.0 - omega[sweep]) / omega[sweep]

                def advance(n, carry):
                    running, x, other = carry
                    i = ROWS - 1 - n if down else n
                    new_running, new_x, new_other = [], [], []
                    values, vs = [], []

                    def finish(c):
                        near = along(vs[c], 1) + along(vs[c], -1)
                        if c:
                            near = near + vs[c - 1]
                        if c < 7:
                            near = near + vs[c + 1]
                        value = scaled[c] * near
                        if keep:
                            value = keep * values[c] + value
                        rho[i, c] = value
                        value_x = value + ratio[c] * x[c]
                        part[i, c] = value_x
                        new_x.append(value_x)
                        new_other.append(other[c] + power[n, c] * value)

                    for c in range(8):
                        value, run, v, _ = solved(n, c, running[c])
                        values.append(value)
                        new_running.append(run)
                        vs.append(v)
                        if c:
                            finish(c - 1)
                    finish(7)
                    return tuple(new_running), tuple(new_x), tuple(new_other)

                _, x, other = lax.fori_loop(0, ROWS, advance, (entering, zeros, zeros), unroll=UNROLL)
                ends, heads = (other, x) if down else (x, other)
            elif step + 1 < DEFECT:

                def renew(n, carry):
                    running, acc = carry
                    i = ROWS - 1 - n if down else n
                    new_running, new_acc = [], []
                    for c in range(8):
                        _, run, _, field = solved(n, c, running[c])
                        new_running.append(run)
                        new_acc.append(acc[c] + mobility(i, c, field))
                    return tuple(new_running), tuple(new_acc)

                total = jnp.stack(lax.fori_loop(0, ROWS, renew, (entering, zeros), unroll=UNROLL)[1])
            else:

                def last(n, running):
                    return tuple(solved(n, c, running[c])[1] for c in range(8))

                lax.fori_loop(0, ROWS, last, entering, unroll=UNROLL)

    kept = tuple(4 * tile + s for tile in range(4) for s in (1, 2))

    def departure(c):
        span = pl.ds(c * 256, 256)
        return pltpu.make_async_copy(sent.at[span], out.at[span], sems.at[3, c])

    def pack(c, carry):
        for upper in range(2):
            for k, (ref, offset) in enumerate(((p, 1), (resid, 0))):
                moved = exchange([ref[upper * GROUP + b + offset, c] for b in range(GROUP)], kept)
                for tile in range(4):
                    for s in range(2):
                        row = (c * 32 + tile * 8) * 8 + s * 4 + k * 2 + upper
                        sent[pl.ds(row, 8, stride=8), :] = moved[4 * tile + 1 + s]
        departure(c).start()
        return carry

    lax.fori_loop(0, 8, pack, 0)
    for c in range(8):
        departure(c).wait()


def unpack_kernel(recv_in, pressure_out, defect_out, recv, pressure, defect, sems):
    def arrival(g):
        span = pl.ds(g * 512, 512)
        return pltpu.make_async_copy(recv_in.at[span], recv.at[span], sems.at[2, g])

    def departures(g):
        for k, (here, there) in enumerate(((pressure, pressure_out), (defect, defect_out))):
            yield pltpu.make_async_copy(here.at[:, tile_span(g)], there.at[:, tile_span(g)], sems.at[k, g])

    for g in range(4):
        arrival(g).start()

    def body(g, carry):
        arrival(g).wait()
        for upper in range(2):
            for k, ref in enumerate((pressure, defect)):
                vectors = []
                for b in range(GROUP):
                    first = 64 * g + 32 * ((b >> 1) & 1) + (b >> 2)
                    row = first * 8 + (b & 1) * 4 + k * 2 + upper
                    vectors.append(recv[pl.ds(row, 8, stride=32), :])
                moved = exchange(snake_sublanes(snake_chunks(vectors)))
                for b in range(GROUP):
                    ref[upper * GROUP + b, tile_span(g), :] = moved[b]
        for copy in departures(g):
            copy.start()
        return carry

    lax.fori_loop(0, 4, body, 0)
    for g in range(4):
        for copy in departures(g):
            copy.wait()


def shape(rows):
    return jax.ShapeDtypeStruct((rows, LANES), jnp.float32)


ANY = pl.BlockSpec(memory_space=pl.ANY)
VMEM = pl.BlockSpec(memory_space=pltpu.VMEM)
SMEM = pl.BlockSpec(memory_space=pltpu.SMEM)


def per_device(pressure, source, facies, mobility_table):
    flat = [x.reshape(ROWS, 32, LANES) for x in (pressure, source, facies)]
    natural = (ROWS, 32, LANES)
    sent = pl.pallas_call(
        pack_kernel,
        out_shape=shape(3072),
        in_specs=[SMEM, ANY, ANY, ANY],
        out_specs=ANY,
        scratch_shapes=[
            pltpu.VMEM(natural, jnp.float32),
            pltpu.VMEM(natural, jnp.float32),
            pltpu.VMEM(natural, jnp.int32),
            pltpu.VMEM((3072, LANES), jnp.float32),
            pltpu.SemaphoreType.DMA((4, 4)),
        ],
        name="pack",
    )(mobility_table, *flat)
    recv = lax.all_to_all(sent.reshape(256, FIELDS, 4, LANES), AXES, 0, 0, tiled=True).reshape(3072, LANES)
    lower, upper = pl.pallas_call(
        halves_kernel,
        out_shape=(shape(1152), shape(1152)),
        in_specs=[ANY],
        out_specs=(ANY, ANY),
        scratch_shapes=[
            pltpu.VMEM((3072, LANES), jnp.float32),
            pltpu.VMEM((1152, LANES), jnp.float32),
            pltpu.VMEM((1152, LANES), jnp.float32),
            pltpu.SemaphoreType.DMA((3, 8)),
        ],
        name="halves",
    )(recv)
    chain = [device_of(t) for t in range(256)]
    right_halo = lax.ppermute(lower, AXES, list(zip(chain[1:], chain[:-1])))
    left_halo = lax.ppermute(upper, AXES, list(zip(chain[:-1], chain[1:])))

    def cells(count):
        return pltpu.VMEM((count,) + SLAB, jnp.float32)

    result = pl.pallas_call(
        work_kernel,
        out_shape=shape(2048),
        in_specs=[ANY, ANY, ANY],
        out_specs=ANY,
        scratch_shapes=[
            cells(ROWS + 2),
            cells(ROWS + 2),
            cells(ROWS + 2),
            cells(ROWS + 2),
            cells(ROWS),
            cells(ROWS),
            cells(ROWS),
            cells(ROWS + 1),
            pltpu.VMEM((3072, LANES), jnp.float32),
            pltpu.VMEM((1152, LANES), jnp.float32),
            pltpu.VMEM((1152, LANES), jnp.float32),
            pltpu.VMEM((2048, LANES), jnp.float32),
            pltpu.SemaphoreType.DMA((4, 8)),
        ],
        name="work",
    )(recv, left_halo, right_halo)
    back = lax.all_to_all(result.reshape(256, 8, LANES), AXES, 0, 0, tiled=True).reshape(2048, LANES)
    outs = pl.pallas_call(
        unpack_kernel,
        out_shape=(jax.ShapeDtypeStruct(natural, jnp.float32),) * 2,
        in_specs=[ANY],
        out_specs=(ANY, ANY),
        scratch_shapes=[
            pltpu.VMEM((2048, LANES), jnp.float32),
            pltpu.VMEM(natural, jnp.float32),
            pltpu.VMEM(natural, jnp.float32),
            pltpu.SemaphoreType.DMA((3, 4)),
        ],
        name="unpack",
    )(back)
    return tuple(x.reshape(pressure.shape) for x in outs)


def solution(mesh):
    spec = P("strike", "cross", None)
    return jax.shard_map(
        per_device,
        mesh=mesh,
        in_specs=(spec, spec, spec, P()),
        out_specs=(spec, spec),
        check_vma=False,
    )
```

```python
import math

import jax
import jax.numpy as jnp
from jax import lax
from jax.experimental import pallas as pl
from jax.experimental.pallas import tpu as pltpu
from jax.sharding import PartitionSpec as P

ND = 1024
CLASSES = 8
DEFECT = 2
SWEEPS = 3

STORE = 0.5
LOW = 0.05
HIGH = 1.95

LANES = 128
BLOCKS = 32
ROWS = ND // BLOCKS
GROUP = 16
AXES = ("cross", "strike")
FIELDS = 3
UNROLL = 4
HALF = 2 * FIELDS


def chebyshev_weights(count):
    middle = 0.5 * (LOW + HIGH)
    half = 0.5 * (HIGH - LOW)
    return [
        1.0 / (middle + half * math.cos(math.pi * (2 * j + 1) / (2 * count))) for j in range(count)
    ]


def device_of(chunk):
    row, q = divmod(chunk, 8)
    z, s = divmod(row, 8)
    if s % 2:
        q = 7 - q
    place = s if s < 4 else 11 - s
    return 64 * z + 4 * place + 32 * (q % 2) + q // 2


def exchange(vectors, keep=range(GROUP)):
    block = lax.broadcasted_iota(jnp.int32, vectors[0].shape, 1) // 8
    vectors = [pltpu.roll(vectors[k], 8 * k, 1) if k else vectors[k] for k in range(GROUP)]
    vectors = [vectors[-k % GROUP] for k in range(GROUP)]
    for step in (1, 2, 4):
        here = (block & step) != 0
        vectors = [jnp.where(here, vectors[(k - step) % GROUP], vectors[k]) for k in range(GROUP)]
    here = block >= 8
    done = {}
    for b in keep:
        moved = jnp.where(here, vectors[(b - 8) % GROUP], vectors[b])
        done[b] = pltpu.roll(moved, LANES - 8 * b, 1) if b else moved
    return done


def snake_sublanes(vectors):
    row = lax.broadcasted_iota(jnp.int32, (8, LANES), 0)
    order = jnp.where(row < 4, row, 11 - row)
    return [jnp.take_along_axis(v, order, axis=0) for v in vectors]


def snake_chunks(vectors):
    row = lax.broadcasted_iota(jnp.int32, (8, LANES), 0)
    odd = ((row & 1) ^ (row >> 2)) != 0
    return [
        jnp.where(odd, vectors[GROUP - 2 - (k & -2) + (k & 1)], vectors[k]) for k in range(GROUP)
    ]


def tile_span(g):
    return pl.ds(pl.multiple_of(g * 8, 8), 8)


def pack_kernel(table, pressure_in, source_in, facies_in, out, pressure, source, facies, sent, sems):
    def arrivals(g):
        pairs = ((pressure_in, pressure), (facies_in, facies), (source_in, source))
        for k, (there, here) in enumerate(pairs):
            yield pltpu.make_async_copy(there.at[:, tile_span(g)], here.at[:, tile_span(g)], sems.at[k, g])

    def departure(g):
        span = pl.ds(g * 128 * HALF, 128 * HALF)
        return pltpu.make_async_copy(sent.at[span], out.at[span], sems.at[3, g])

    def lookup(codes):
        base = jnp.zeros(codes.shape, jnp.float32)
        for code in range(CLASSES):
            base = jnp.where(codes == code, table[code], base)
        return base

    for g in range(4):
        for copy in arrivals(g):
            copy.start()

    def body(g, carry):
        for copy in arrivals(g):
            copy.wait()
        for upper in range(2):

            def read(ref):
                return [ref[upper * GROUP + b, tile_span(g), :] for b in range(GROUP)]

            fields = (read(pressure), [lookup(c) for c in read(facies)], read(source))
            for k, vectors in enumerate(fields):
                moved = snake_chunks(exchange(snake_sublanes(vectors)))
                for b in range(GROUP):
                    first = 64 * g + 32 * ((b >> 1) & 1) + (b >> 2)
                    row = first * 2 * HALF + (b & 1) * HALF + k * 2 + upper
                    sent[pl.ds(row, 8, stride=8 * HALF), :] = moved[b]
        departure(g).start()
        return carry

    lax.fori_loop(0, 4, body, 0)
    for g in range(4):
        departure(g).wait()


def cell_index():
    return lax.broadcasted_iota(jnp.int32, (8, LANES), 1) % 8


def squeeze(four, tail):
    cell = cell_index()
    free = cell < 2 if tail else cell >= 6
    sign = -1 if tail else 1
    shifts = (2, 4, 6) if tail else (6, 4, 2)
    return [jnp.where(free, pltpu.roll(four[3], sign * n % LANES, 1), v) for v, n in zip(four, shifts)]


def stretch(three, tail):
    cell = cell_index()
    if tail:
        a, b, c = (pltpu.roll(v, n, 1) for v, n in zip(three, (2, 4, 6)))
        return list(three) + [jnp.where(cell >= 6, c, jnp.where(cell >= 4, b, a))]
    a, b, c = (pltpu.roll(v, LANES - n, 1) for v, n in zip(three, (6, 4, 2)))
    return list(three) + [jnp.where(cell < 2, a, jnp.where(cell < 4, b, c))]


def halves_kernel(recv, lower, upper, whole, first, second, sems):
    def arrival(c):
        span = pl.ds(c * 64 * HALF, 64 * HALF)
        return pltpu.make_async_copy(recv.at[span], whole.at[span], sems.at[2, c])

    def departure(c, side):
        span = pl.ds(c * 24 * HALF, 24 * HALF)
        return pltpu.make_async_copy((first, second)[side].at[span], (lower, upper)[side].at[span], sems.at[side, c])

    for c in range(8):
        arrival(c).start()

    def body(c, carry):
        arrival(c).wait()
        for side, ref in enumerate((first, second)):
            for w in range(HALF):
                four = [
                    whole[pl.ds((c * 32 + tile * 8) * 2 * HALF + side * HALF + w, 8, stride=2 * HALF), :]
                    for tile in range(4)
                ]
                for n, vector in enumerate(squeeze(four, side == 1)):
                    ref[pl.ds((c * HALF + w) * 24 + n * 8, 8), :] = vector
            departure(c, side).start()
        return carry

    lax.fori_loop(0, 8, body, 0, unroll=2)
    for c in range(8):
        for side in range(2):
            departure(c, side).wait()


SLAB = (8, 8, LANES)


def roll_lanes(x, shift):
    return pltpu.roll(x.reshape(64, LANES), shift % LANES, 1).reshape(x.shape)


def shift_blocks(x, shift):
    lane = lax.broadcasted_iota(jnp.int32, SLAB, 2)
    if abs(shift) >= 8:
        lanes = shift * 4
        keep = (lane >= lanes) if shift > 0 else (lane < LANES + lanes)
        return jnp.where(keep, roll_lanes(x, lanes), 0.0)
    sub = lax.broadcasted_iota(jnp.int32, SLAB, 1)
    near = jnp.stack([pltpu.roll(x[c], shift % 8, 0) for c in range(8)])
    if shift > 0:
        far = jnp.where(lane >= 32, roll_lanes(near, 32), 0.0)
        return jnp.where(sub >= shift, near, far)
    far = jnp.where(lane < 96, roll_lanes(near, -32), 0.0)
    return jnp.where(sub < 8 + shift, near, far)


def column_sum(x):
    total = jnp.broadcast_to(jnp.sum(x, axis=1, keepdims=True), SLAB)
    total = total + roll_lanes(total, 32)
    return total + roll_lanes(total, 64)


def roll_sublanes(x, shift):
    return jnp.stack([pltpu.roll(x[c], shift % 8, 0) for c in range(8)])


def work_kernel(
    own_in, left_in, right_in, out, p, m, base, source, resid, rho, part, power, own, left, right, sent, sems
):
    omega = chebyshev_weights(SWEEPS)
    fields = (p, base, source)

    def arrivals(c):
        for k, (there, here, rows) in enumerate(
            ((own_in, own, 64 * HALF), (left_in, left, 24 * HALF), (right_in, right, 24 * HALF))
        ):
            span = pl.ds(c * rows, rows)
            yield pltpu.make_async_copy(there.at[span], here.at[span], sems.at[k, c])

    for c in range(8):
        for copy in arrivals(c):
            copy.start()

    def unpack(c, carry):
        for copy in arrivals(c):
            copy.wait()
        for upper in range(2):
            for k in range(FIELDS):
                vectors = []
                w = k * 2 + upper
                first = (c * HALF + w) * 24
                before = stretch([left[pl.ds(first + n * 8, 8), :] for n in range(3)], True)
                after = stretch([right[pl.ds(first + n * 8, 8), :] for n in range(3)], False)
                for tile in range(4):
                    block = c * 32 + tile * 8
                    vectors.append(before[tile])
                    vectors.append(own[pl.ds(block * 2 * HALF + w, 8, stride=2 * HALF), :])
                    vectors.append(own[pl.ds(block * 2 * HALF + HALF + w, 8, stride=2 * HALF), :])
                    vectors.append(after[tile])
                moved = exchange(vectors)
                for b in range(GROUP):
                    fields[k][upper * GROUP + b + 1, c] = moved[b]
        return carry

    lax.fori_loop(0, 8, unpack, 0)

    lane = lax.broadcasted_iota(jnp.int32, SLAB, 2)
    sub = lax.broadcasted_iota(jnp.int32, SLAB, 1)

    zeros = tuple(jnp.zeros((8, LANES), jnp.float32) for _ in range(8))

    def mobility(i, c, field):
        value = base[i + 1, c] * (0.5 + 0.25 * jnp.tanh(field))
        m[i + 1, c] = value
        return value

    def start(i, acc):
        return tuple(acc[c] + mobility(i, c, p[i + 1, c]) for c in range(8))

    total = jnp.stack(lax.fori_loop(0, ROWS, start, zeros, unroll=UNROLL))

    for step in range(DEFECT):
        for ref in (p, m):
            ref[0] = shift_blocks(ref[ROWS], 1)
            ref[ROWS + 1] = shift_blocks(ref[1], -1)

        mref = column_sum(total) * (2.0 / ND)
        inside = mref > 0.0
        safe = jnp.where(inside, mref, 1.0)
        half = 0.5 * (4.0 + STORE / safe)
        ratio = 1.0 / (1.0 + half + jnp.sqrt(half * (half + 2.0)))
        gain = ratio / ((1.0 - ratio * ratio) * safe)
        inner = gain * mref
        gain = jnp.where(inside, gain, 0.0)

        def powers(i, value):
            power[i] = value
            return value * ratio

        block_ratio = lax.fori_loop(0, ROWS, powers, jnp.ones(SLAB, jnp.float32), unroll=4)
        power[ROWS] = block_ratio
        squares = [block_ratio]
        for _ in range(5):
            squares.append(squares[-1] * squares[-1])
        whole = squares[5]
        reflect = 1.0 / (1.0 - whole * whole)
        below_sub = jnp.ones(SLAB, jnp.float32)
        above_sub = jnp.ones(SLAB, jnp.float32)
        for bit in range(3):
            on = ((sub >> bit) & 1) != 0
            below_sub = jnp.where(on, below_sub * squares[bit], below_sub)
            above_sub = jnp.where(on, above_sub, above_sub * squares[bit])
        from_left, from_right = below_sub, above_sub
        for bit in range(2):
            on = ((lane >> (5 + bit)) & 1) != 0
            from_left = jnp.where(on, from_left * squares[3 + bit], from_left)
            from_right = jnp.where(on, from_right, from_right * squares[3 + bit])

        def spread(x, kept):
            x = jnp.where(kept, x, 0.0)
            x = x + roll_lanes(x, 32)
            return x + roll_lanes(x, 64)

        def carries(ends, heads):
            for bit in range(3):
                s = 1 << bit
                ends = ends + squares[bit] * jnp.where(sub >= s, roll_sublanes(ends, s), 0.0)
                heads = heads + squares[bit] * jnp.where(sub < 8 - s, roll_sublanes(heads, -s), 0.0)
            end = jnp.broadcast_to(ends[:, 7:8], SLAB)
            head = jnp.broadcast_to(heads[:, 0:1], SLAB)
            before, after = shift_blocks(end, 8), shift_blocks(head, -8)
            before = before + squares[3] * shift_blocks(before, 8)
            after = after + squares[3] * shift_blocks(after, -8)
            before = before + squares[4] * shift_blocks(before, 16)
            after = after + squares[4] * shift_blocks(after, -16)
            a = spread(head + squares[3] * after, lane < 32)
            b = spread(end + squares[3] * before, lane >= 96)
            before = jnp.where(sub > 0, roll_sublanes(ends, 1), 0.0) + below_sub * before
            after = jnp.where(sub < 7, roll_sublanes(heads, -1), 0.0) + above_sub * after
            before = before + from_left * ((a + whole * b) * reflect)
            after = after + from_right * ((b + whole * a) * reflect)
            return before, after

        first_gain = omega[0] * gain

        def along(x, shift):
            return pltpu.roll(x, shift % LANES, 1)

        def form(i, carry):
            y, other, above = carry
            here = [p[i + 1, c] for c in range(8)]
            mob = [m[i + 1, c] for c in range(8)]
            new_y, new_other, new_above = [], [], []
            left = mob[0] * -here[0]
            for c in range(8):
                below = (mob[c] + m[i + 2, c]) * (here[c] - p[i + 2, c])
                if c < 7:
                    right = (mob[c] + mob[c + 1]) * (here[c] - here[c + 1])
                else:
                    right = mob[c] * here[c]
                strike = (mob[c] + along(mob[c], -1)) * (here[c] - along(here[c], -1))
                flow = (below - above[c]) + (right - left) + (strike - along(strike, 1))
                left = right
                result = (source[i + 1, c] - STORE * here[c]) - flow
                if step + 1 == DEFECT:
                    resid[i, c] = result
                value = first_gain[c] * result
                rho[i, c] = value
                value_y = value + ratio[c] * y[c]
                part[i, c] = value_y
                new_y.append(value_y)
                new_other.append(other[c] + power[i, c] * value)
                new_above.append(below)
            return tuple(new_y), tuple(new_other), tuple(new_above)

        first = tuple((m[0, c] + m[1, c]) * (p[0, c] - p[1, c]) for c in range(8))
        ends, heads, _ = lax.fori_loop(0, ROWS, form, (zeros, zeros, first), unroll=UNROLL)
        for sweep in range(SWEEPS):
            before, after = carries(jnp.stack(ends), jnp.stack(heads))
            down = sweep % 2 == 0
            entering, stored = (after, before) if down else (before, after)
            entering = tuple(entering[c] for c in range(8))

            def solved(n, c, running):
                i = ROWS - 1 - n if down else n
                value = rho[i, c]
                opposite = ratio[c] * running
                v = (part[i, c] + opposite) + power[ROWS - n, c] * stored[c]
                field = p[i + 1, c] + v
                p[i + 1, c] = field
                return value, value + opposite, v, field

            if sweep + 1 < SWEEPS:
                scaled = omega[sweep + 1] * inner
                keep = omega[sweep + 1] * (1.0 - omega[sweep]) / omega[sweep]

                def advance(n, carry):
                    running, x, other = carry
                    i = ROWS - 1 - n if down else n
                    new_running, new_x, new_other = [], [], []
                    values, vs = [], []

                    def finish(c):
                        near = along(vs[c], 1) + along(vs[c], -1)
                        if c:
                            near = near + vs[c - 1]
                        if c < 7:
                            near = near + vs[c + 1]
                        value = scaled[c] * near
                        if keep:
                            value = keep * values[c] + value
                        rho[i, c] = value
                        value_x = value + ratio[c] * x[c]
                        part[i, c] = value_x
                        new_x.append(value_x)
                        new_other.append(other[c] + power[n, c] * value)

                    for c in range(8):
                        value, run, v, _ = solved(n, c, running[c])
                        values.append(value)
                        new_running.append(run)
                        vs.append(v)
                        if c:
                            finish(c - 1)
                    finish(7)
                    return tuple(new_running), tuple(new_x), tuple(new_other)

                _, x, other = lax.fori_loop(0, ROWS, advance, (entering, zeros, zeros), unroll=UNROLL)
                ends, heads = (other, x) if down else (x, other)
            elif step + 1 < DEFECT:

                def renew(n, carry):
                    running, acc = carry
                    i = ROWS - 1 - n if down else n
                    new_running, new_acc = [], []
                    for c in range(8):
                        _, run, _, field = solved(n, c, running[c])
                        new_running.append(run)
                        new_acc.append(acc[c] + mobility(i, c, field))
                    return tuple(new_running), tuple(new_acc)

                total = jnp.stack(lax.fori_loop(0, ROWS, renew, (entering, zeros), unroll=UNROLL)[1])
            else:

                def last(n, running):
                    return tuple(solved(n, c, running[c])[1] for c in range(8))

                lax.fori_loop(0, ROWS, last, entering, unroll=UNROLL)

    kept = tuple(4 * tile + s for tile in range(4) for s in (1, 2))

    def departure(c):
        span = pl.ds(c * 256, 256)
        return pltpu.make_async_copy(sent.at[span], out.at[span], sems.at[3, c])

    def pack(c, carry):
        for upper in range(2):
            for k, (ref, offset) in enumerate(((p, 1), (resid, 0))):
                moved = exchange([ref[upper * GROUP + b + offset, c] for b in range(GROUP)], kept)
                for tile in range(4):
                    for s in range(2):
                        row = (c * 32 + tile * 8) * 8 + s * 4 + k * 2 + upper
                        sent[pl.ds(row, 8, stride=8), :] = moved[4 * tile + 1 + s]
        departure(c).start()
        return carry

    lax.fori_loop(0, 8, pack, 0)
    for c in range(8):
        departure(c).wait()


def unpack_kernel(recv_in, pressure_out, defect_out, recv, pressure, defect, sems):
    def arrival(g):
        span = pl.ds(g * 512, 512)
        return pltpu.make_async_copy(recv_in.at[span], recv.at[span], sems.at[2, g])

    def departures(g):
        for k, (here, there) in enumerate(((pressure, pressure_out), (defect, defect_out))):
            yield pltpu.make_async_copy(here.at[:, tile_span(g)], there.at[:, tile_span(g)], sems.at[k, g])

    for g in range(4):
        arrival(g).start()

    def body(g, carry):
        arrival(g).wait()
        for upper in range(2):
            for k, ref in enumerate((pressure, defect)):
                vectors = []
                for b in range(GROUP):
                    first = 64 * g + 32 * ((b >> 1) & 1) + (b >> 2)
                    row = first * 8 + (b & 1) * 4 + k * 2 + upper
                    vectors.append(recv[pl.ds(row, 8, stride=32), :])
                moved = exchange(snake_sublanes(snake_chunks(vectors)))
                for b in range(GROUP):
                    ref[upper * GROUP + b, tile_span(g), :] = moved[b]
        for copy in departures(g):
            copy.start()
        return carry

    lax.fori_loop(0, 4, body, 0)
    for g in range(4):
        for copy in departures(g):
            copy.wait()


def shape(rows):
    return jax.ShapeDtypeStruct((rows, LANES), jnp.float32)


ANY = pl.BlockSpec(memory_space=pl.ANY)
VMEM = pl.BlockSpec(memory_space=pltpu.VMEM)
SMEM = pl.BlockSpec(memory_space=pltpu.SMEM)


def per_device(pressure, source, facies, mobility_table):
    flat = [x.reshape(ROWS, 32, LANES) for x in (pressure, source, facies)]
    natural = (ROWS, 32, LANES)
    sent = pl.pallas_call(
        pack_kernel,
        out_shape=shape(3072),
        in_specs=[SMEM, ANY, ANY, ANY],
        out_specs=ANY,
        scratch_shapes=[
            pltpu.VMEM(natural, jnp.float32),
            pltpu.VMEM(natural, jnp.float32),
            pltpu.VMEM(natural, jnp.int32),
            pltpu.VMEM((3072, LANES), jnp.float32),
            pltpu.SemaphoreType.DMA((4, 4)),
        ],
        name="pack",
    )(mobility_table, *flat)
    recv = lax.all_to_all(sent.reshape(256, FIELDS, 4, LANES), AXES, 0, 0, tiled=True).reshape(3072, LANES)
    lower, upper = pl.pallas_call(
        halves_kernel,
        out_shape=(shape(1152), shape(1152)),
        in_specs=[ANY],
        out_specs=(ANY, ANY),
        scratch_shapes=[
            pltpu.VMEM((3072, LANES), jnp.float32),
            pltpu.VMEM((1152, LANES), jnp.float32),
            pltpu.VMEM((1152, LANES), jnp.float32),
            pltpu.SemaphoreType.DMA((3, 8)),
        ],
        name="halves",
    )(recv)
    chain = [device_of(t) for t in range(256)]
    right_halo = lax.ppermute(lower, AXES, list(zip(chain[1:], chain[:-1])))
    left_halo = lax.ppermute(upper, AXES, list(zip(chain[:-1], chain[1:])))

    def cells(count):
        return pltpu.VMEM((count,) + SLAB, jnp.float32)

    result = pl.pallas_call(
        work_kernel,
        out_shape=shape(2048),
        in_specs=[ANY, ANY, ANY],
        out_specs=ANY,
        scratch_shapes=[
            cells(ROWS + 2),
            cells(ROWS + 2),
            cells(ROWS + 2),
            cells(ROWS + 2),
            cells(ROWS),
            cells(ROWS),
            cells(ROWS),
            cells(ROWS + 1),
            pltpu.VMEM((3072, LANES), jnp.float32),
            pltpu.VMEM((1152, LANES), jnp.float32),
            pltpu.VMEM((1152, LANES), jnp.float32),
            pltpu.VMEM((2048, LANES), jnp.float32),
            pltpu.SemaphoreType.DMA((4, 8)),
        ],
        name="work",
    )(recv, left_halo, right_halo)
    back = lax.all_to_all(result.reshape(256, 8, LANES), AXES, 0, 0, tiled=True).reshape(2048, LANES)
    outs = pl.pallas_call(
        unpack_kernel,
        out_shape=(jax.ShapeDtypeStruct(natural, jnp.float32),) * 2,
        in_specs=[ANY],
        out_specs=(ANY, ANY),
        scratch_shapes=[
            pltpu.VMEM((2048, LANES), jnp.float32),
            pltpu.VMEM(natural, jnp.float32),
            pltpu.VMEM(natural, jnp.float32),
            pltpu.SemaphoreType.DMA((3, 4)),
        ],
        name="unpack",
    )(back)
    return tuple(x.reshape(pressure.shape) for x in outs)


def solution(mesh):
    spec = P("strike", "cross", None)
    return jax.shard_map(
        per_device,
        mesh=mesh,
        in_specs=(spec, spec, spec, P()),
        out_specs=(spec, spec),
        check_vma=False,
    )
```
